32 devices in a mesh: groups: 2 (over y), rx: 8 (over z, x), xl: 2 (over core).
Axes of the slice: x: 2, y: 2, z: 4, core: 2. Of those that a mesh axis runs over, the one named last changes fastest.
Arguments:
- source_traces: bfloat16 [4, 512, 2048], P(None, ('groups', 'rx', 'xl')), parts along dimension 1, may hold values from -6 to 6
- surface_filter: float32 [2, 1024], replicated, may hold values from -6 to 6
- records: bfloat16 [8192, 2048], P(('groups', 'rx', 'xl')), parts along dimension 0, may hold values from -6 to 6
- owners: int32 [8192], P(('groups', 'rx', 'xl')), parts along dimension 0, may hold values from 0 to 1, as said below
- aperture: int32 [64, 128], P(('groups', 'rx', 'xl')), parts along dimension 0, may hold values from 0 to 255, as said below
Outputs:
- multiples: bfloat16 [4, 64, 2048], P(None, ('groups', 'rx', 'xl')), parts along dimension 1
The draws below stay inside these ranges and needn't reach their ends.
There are 2 independent parts, one for each index of `groups`. The reference program is written for one: setup_inputs(seed, part) draws one part's arguments, and reference() takes and returns one part's arrays. A program takes and returns all parts, laid end to end along the dimension named above; an argument that names none is the same for every part. Nothing has to cross between parts.
Inputs may be any that keep to these rules, and one draw needn't show every extreme that they name: owners holds the xl index of the destination, which has the same rx index as the record's device. Every owner receives exactly 256 records, at most 192 from one device, and in every draw some device sends exactly 192 records to one owner. `aperture`: the 128 indices of one output trace are distinct.
All inputs are finite; a program needn't handle non-finite values.
Results may differ from the reference program's by a relative error of at most 0.008.
Values may be sent and summed in bfloat16 or wider, within the bound.
No kernel may reach another device: no remote copies, remote signals or barrier semaphores. Data moves between devices by JAX's collectives and lax.ppermute only.
A program may use at most 128 MiB of HBM per device.

```python
import math
import jax
import jax.numpy as jnp
from jax import lax

SOURCES = 4
SAMPLES = 2048
FREQS = 1024
GATHER = 256
APER = 128
OUT_DEV = 2
REC_DEV = 256
OUTS = 32
RECORDS = 4096


def draw_owners(key, part):
    pairs = RECORDS // (2 * REC_DEV)
    bound = REC_DEV - REC_DEV // 4
    lowest = REC_DEV - bound
    key_counts, key_scores = jax.random.split(key)
    first = jax.random.randint(key_counts, (pairs,), lowest, bound + 1)
    first = first.at[0].set(bound).at[1].set(lowest)
    to_zero = jnp.stack([first, REC_DEV - first], axis=1).reshape(-1)
    scores = jax.random.randint(key_scores, (pairs * 2, REC_DEV), 0, 65536) * REC_DEV
    scores = scores + jnp.arange(REC_DEV, dtype=jnp.int32)[None, :]
    ranking = jnp.argsort(jnp.argsort(scores, axis=1), axis=1)
    return jnp.where(ranking < to_zero[:, None], 0, 1).astype(jnp.int32).reshape(-1)


def draw_aperture(key, part):
    scores = jax.random.randint(key, (OUTS, GATHER), 0, 65536) * GATHER
    scores = scores + jnp.arange(GATHER, dtype=jnp.int32)[None, :]
    ordering = jnp.argsort(scores, axis=1)
    return ordering[:, :APER].astype(jnp.int32)


def steps_of(rng, dims, cuts, smallest, largest):
    factor_of, own = 1.0, jax.random.fold_in(rng, 6)
    for dim, blocks in cuts:
        steps = jnp.exp(jax.random.uniform(jax.random.fold_in(own, dim), (blocks,), jnp.float32, smallest / len(cuts), largest / len(cuts)))
        factor_of = factor_of * jnp.repeat(steps, dims[dim] // blocks).reshape([-1 if axis == dim else 1 for axis in range(len(dims))])
    return factor_of


def centred(own_key, dims, scale, reach, cuts=(), held_as=jnp.bfloat16):
    entries = scale * jax.random.normal(own_key, dims, jnp.float32)
    if cuts:
        entries = entries * steps_of(own_key, dims, cuts, -0.22, 0.18)
    return jnp.clip(entries, -reach, reach).astype(held_as)


def setup_inputs(seed: int = 0, part: int = 0) -> dict:
    streams_of = jax.random.split(jax.random.key(seed), 6)
    part_keys = jax.random.split(jax.random.fold_in(streams_of[5], part), 6)
    return {
        "source_traces": centred(part_keys[0], (SOURCES, GATHER, SAMPLES), 1.0, 6.0, ((1, 16),)),
        "surface_filter": centred(streams_of[1], (2, FREQS), 1.0, 6.0, (), jnp.float32),
        "records": centred(part_keys[2], (RECORDS, SAMPLES), 1.0, 6.0, ((0, 16),)),
        "owners": draw_owners(jax.random.fold_in(jax.random.fold_in(streams_of[5], part), 71), part),
        "aperture": draw_aperture(jax.random.fold_in(jax.random.fold_in(streams_of[5], part), 71), part),
    }


def forward_table(samples, first, count):
    times = jnp.arange(samples, dtype=jnp.int32)[:, None]
    waves = (first + jnp.arange(count, dtype=jnp.int32))[None, :]
    phase = (times * waves % samples).astype(jnp.float32) * (2.0 * math.pi / samples)
    factor = 1.0 / math.sqrt(samples)
    return ((jnp.cos(phase) * factor).astype(jnp.bfloat16), (-jnp.sin(phase) * factor).astype(jnp.bfloat16))

def inverse_table(samples, first, count):
    frequencies = samples // 2
    waves = jnp.arange(frequencies, dtype=jnp.int32)[:, None]
    times = (first + jnp.arange(count, dtype=jnp.int32))[None, :]
    phase = (times * waves % samples).astype(jnp.float32) * (2.0 * math.pi / samples)
    factor = 1.0 / math.sqrt(frequencies)
    return jnp.concatenate([jnp.cos(phase) * factor, -jnp.sin(phase) * factor], axis=0).astype(jnp.bfloat16)

def transform(traces, samples):
    frequencies = samples // 2
    width = min(256, frequencies)
    real_list = []
    imag_list = []
    for first in range(0, frequencies, width):
        cosine, sine = forward_table(samples, first, width)
        real_list.append(jnp.dot(traces, cosine, preferred_element_type=jnp.float32))
        imag_list.append(jnp.dot(traces, sine, preferred_element_type=jnp.float32))
    return jnp.concatenate(real_list + imag_list, axis=1).astype(jnp.bfloat16)

def untransform(spectra, samples):
    width = min(256, samples)
    pieces = []
    for first in range(0, samples, width):
        pieces.append(jnp.dot(spectra, inverse_table(samples, first, width), preferred_element_type=jnp.float32))
    return jnp.concatenate(pieces, axis=1).astype(jnp.bfloat16)

def convolve(source_spectra, record_spectra, columns):
    frequencies = record_spectra.shape[-1] // 2
    right_real = record_spectra[..., :frequencies].astype(jnp.float32)
    right_imaginary = record_spectra[..., frequencies:].astype(jnp.float32)
    results = []
    for source_index in range(source_spectra.shape[0]):
        picked = jnp.take(source_spectra[source_index], columns, axis=0)
        left_real = picked[..., :frequencies].astype(jnp.float32)
        left_imaginary = picked[..., frequencies:].astype(jnp.float32)
        real_part = lax.optimization_barrier(jnp.sum(left_real * right_real - left_imaginary * right_imaginary, axis=1))
        imaginary = lax.optimization_barrier(jnp.sum(left_real * right_imaginary + left_imaginary * right_real, axis=1))
        results.append(jnp.concatenate([real_part, imaginary], axis=1))
    return jnp.stack(results, axis=0)

def apply_filter(raw, surface_filter, aperture_length):
    frequencies = raw.shape[-1] // 2
    factor = 1.0 / math.sqrt(aperture_length)
    raw_real = raw[..., :frequencies]
    raw_imaginary = raw[..., frequencies:]
    filter_real = surface_filter[0] * factor
    filter_imaginary = surface_filter[1] * factor
    real_part = filter_real * raw_real - filter_imaginary * raw_imaginary
    imaginary = filter_real * raw_imaginary + filter_imaginary * raw_real
    return jnp.concatenate([real_part, imaginary], axis=-1).astype(jnp.bfloat16)

def reference(source_traces, surface_filter, records, owners, aperture):
    sources, traces, samples = source_traces.shape
    source_spectra = transform(source_traces.reshape(sources * traces, samples), samples).reshape(sources, traces, samples)
    pair_rows = 2 * REC_DEV
    pairs = records.shape[0] // pair_rows
    pair_records = records.reshape(pairs, pair_rows, samples)
    pair_owners = owners.reshape(pairs, pair_rows)
    pair_aperture = aperture.reshape(pairs, 2 * OUT_DEV, APER)

    def one_pair(items):
        block, destinations, columns = items
        position = jnp.arange(pair_rows, dtype=jnp.int32)
        ordering = jnp.argsort(destinations * pair_rows + position).astype(jnp.int32)
        routed = jnp.take(block, ordering, axis=0)
        record_spectra = transform(routed, samples).reshape(2 * OUT_DEV, APER, samples)
        raw = convolve(source_spectra, record_spectra, columns)
        filtered = apply_filter(raw, surface_filter, APER)
        flat = untransform(filtered.reshape(sources * 2 * OUT_DEV, samples), samples)
        return flat.reshape(sources, 2 * OUT_DEV, samples)
    mapped = lax.map(one_pair, (pair_records, pair_owners, pair_aperture))
    return jnp.transpose(mapped, (1, 0, 2, 3)).reshape(sources, pairs * 2 * OUT_DEV, samples)
```

```python
import functools
import math

import jax
import jax.numpy as jnp
import numpy as np
from jax import lax
from jax.experimental import pallas as pl
from jax.experimental.pallas import tpu as pltpu
from jax.sharding import PartitionSpec as P

F32, BF16, I32 = jnp.float32, jnp.bfloat16, jnp.int32
ROWS = 16
STEP = 32


def small_tables(samples):
    half, quarter = samples // 2, samples // 4
    unit = 2.0 * math.pi / samples

    def pair(a, b, factor):
        phase = (a * b % samples) * unit
        return [np.cos(phase) * factor, np.sin(phase) * factor]

    waves = 2 * np.arange(quarter)[None, None, :] + np.arange(2)[:, None, None]
    coarse = STEP * np.arange(half // STEP)[None, :, None]
    fine = np.arange(STEP)[None, :, None]
    forward_coarse = np.stack(pair(coarse, waves, 1.0), axis=1)
    forward_fine = np.stack(pair(fine, waves, 1.0 / math.sqrt(samples)), axis=1)
    times = np.arange(half)[None, :]
    steps = 2 * STEP * np.arange(quarter // STEP)[:, None]
    inverse_coarse = np.stack(pair(steps, times, 1.0))
    firsts = 2 * np.arange(STEP)[None, :, None] + np.arange(2)[:, None, None]
    inverse_fine = np.stack(pair(firsts, times[None], 1.0 / math.sqrt(half)), axis=1)
    return [
        a.astype(np.float32)
        for a in (forward_coarse, forward_fine, inverse_coarse, inverse_fine)
    ]


def forward_tables_kernel(coarse, fine, out):
    quarter = coarse.shape[-1]

    def step(i, carry):
        for p in range(2):
            c1 = coarse[p, 0, pl.ds(i, 1), :]
            s1 = coarse[p, 1, pl.ds(i, 1), :]
            c0, s0 = fine[p, 0], fine[p, 1]
            rows = pl.ds(i * STEP, STEP)
            out[p, rows, :quarter] = (c1 * c0 - s1 * s0).astype(BF16)
            out[p, rows, quarter:] = (-(s1 * c0) - c1 * s0).astype(BF16)
        return carry

    lax.fori_loop(0, out.shape[1] // STEP, step, 0)


def inverse_tables_kernel(coarse, fine, out):
    quarter = out.shape[1] // 2

    def step(i, carry):
        c1 = coarse[0, pl.ds(i, 1), :]
        s1 = coarse[1, pl.ds(i, 1), :]
        for p in range(2):
            c0, s0 = fine[p, 0], fine[p, 1]
            out[p, pl.ds(i * STEP, STEP), :] = (c1 * c0 - s1 * s0).astype(BF16)
            out[p, pl.ds(quarter + i * STEP, STEP), :] = (-(s1 * c0) - c1 * s0).astype(BF16)
        return carry

    lax.fori_loop(0, quarter // STEP, step, 0)


def butterfly(x):
    half = x.shape[-1] // 2
    first, second = x[:, :half].astype(F32), x[:, half:].astype(F32)
    return (first + second).astype(BF16), (first - second).astype(BF16)


def records_kernel(per_device, aper, where, own, other, tags, tables, out):
    core = where[1]
    rec_dev = own.shape[0]
    slots = 2 * rec_dev
    outs = slots // aper
    earlier = (
        lax.broadcasted_iota(I32, (rec_dev, rec_dev), 0)
        < lax.broadcasted_iota(I32, (rec_dev, rec_dev), 1)
    ).astype(F32).astype(BF16)
    picks = []
    ranks, totals, owners = [], [], []
    for side in range(2):
        owner = tags[side : side + 1, :]
        zero = (owner == 0).astype(F32)
        rank = jnp.dot(
            jnp.broadcast_to(zero, (8, rec_dev)).astype(BF16), earlier, preferred_element_type=F32
        )[:1]
        ranks.append(rank)
        totals.append(jnp.sum(zero, axis=1, keepdims=True))
        owners.append(owner)
    position = lax.broadcasted_iota(I32, (1, rec_dev), 1)
    slot_row = lax.broadcasted_iota(I32, (slots, rec_dev), 0)
    for side in range(2):
        second = (core == 0) if side == 1 else (core == 1)
        before = jnp.where(second, totals[1 - side], 0.0)
        zeros = (ranks[side] + before).astype(I32)
        place = position + jnp.where(second, rec_dev, 0)
        slot = jnp.where(owners[side] == 0, zeros, rec_dev + place - zeros)
        picks.append((slot_row == slot).astype(F32).astype(BF16))
    trace = lax.broadcasted_iota(I32, (aper, aper), 0)
    trace = trace // per_device * (2 * per_device) + core * per_device + trace % per_device
    rows = []
    for r in range(outs):
        entries = tags[2 + r : 3 + r, :aper]
        match = (trace == entries).astype(F32).astype(BF16)
        rows.append(
            [
                jnp.dot(
                    match, picks[side][r * aper : (r + 1) * aper], preferred_element_type=F32
                ).astype(BF16)
                for side in range(2)
            ]
        )
    place_own = jnp.concatenate([a for a, _ in rows], axis=0)
    place_other = jnp.concatenate([b for _, b in rows], axis=0)
    routed = jnp.dot(place_own, own[...], preferred_element_type=F32) + jnp.dot(
        place_other, other[...], preferred_element_type=F32
    )
    half = routed.shape[1] // 2
    even = (routed[:, :half] + routed[:, half:]).astype(BF16)
    odd = (routed[:, :half] - routed[:, half:]).astype(BF16)
    chunks = aper // ROWS
    for p, data in enumerate((even, odd)):
        result = jnp.dot(data, tables[p], preferred_element_type=F32)
        out[:, :, :, p * half : (p + 1) * half] = result.reshape(outs, chunks, ROWS, half)


def ring_chunk(where, offset):
    me = where[0]
    place = jnp.where(me % 2 == 0, me // 2, 7 - me // 2)
    place = (place + offset) % 8
    return jnp.where(place < 4, 2 * place, 15 - 2 * place)


def products_kernel(offsets, ringed, with_total, where, *refs):
    count = len(offsets)
    pieces = refs[:count]
    tables, spectra = refs[count : count + 2]
    rest = refs[count + 2 :]
    total_in = rest[0] if with_total else None
    rest = rest[1:] if with_total else rest
    outs, work = rest[:-1], rest[-1]
    sources = pieces[0].shape[0]
    half = tables.shape[1]
    quarter = half // 2
    data = [butterfly(x[...].reshape(-1, 2 * half)) for x in pieces]
    rows = data[0][0].shape[0]
    for p in range(2):
        joined = jnp.concatenate([d[p] for d in data], axis=0) if count > 1 else data[0][p]
        work[:, p * half : (p + 1) * half] = jnp.dot(
            joined, tables[p], preferred_element_type=F32
        )
    chunk = [ring_chunk(where, offset) if ringed else offset for offset in offsets]
    number = spectra.shape[0]
    total = outs[0]
    for p in range(2):
        for block in range(quarter // 128):
            re = pl.ds(p * half + block * 128, 128)
            im = pl.ds(p * half + quarter + block * 128, 128)
            sums = {}
            for c in range(count):
                for h in range(ROWS // 8):
                    left = []
                    for s in range(sources):
                        first = c * rows + s * ROWS + h * 8
                        left.append((work[first : first + 8, re], work[first : first + 8, im]))
                    for r in range(number):
                        b_re = spectra[r, chunk[c], h * 8 : h * 8 + 8, re]
                        b_im = spectra[r, chunk[c], h * 8 : h * 8 + 8, im]
                        for s in range(sources):
                            a_re, a_im = left[s]
                            x = a_re * b_re - a_im * b_im
                            y = a_re * b_im + a_im * b_re
                            if (s, r) in sums:
                                x, y = x + sums[s, r][0], y + sums[s, r][1]
                            sums[s, r] = (x, y)
            for (s, r), (x, y) in sums.items():
                if with_total:
                    x, y = x + total_in[s, r, :, re], y + total_in[s, r, :, im]
                total[s, r, :, re] = x
                total[s, r, :, im] = y


def reduce_kernel(where, total, mine, theirs):
    core = where[1]
    for s in range(total.shape[0]):
        for r in range(2):
            mine[2 * s + r : 2 * s + r + 1, :] = jnp.sum(
                total[s, 2 * core + r], axis=0, keepdims=True
            )
            theirs[2 * s + r : 2 * s + r + 1, :] = jnp.sum(
                total[s, 2 - 2 * core + r], axis=0, keepdims=True
            )


def finish_kernel(scale, filters, mine, arrived, tables, out):
    half = tables.shape[1]
    quarter = half // 2
    raw = mine[...] + arrived[...]
    parts = []
    for p in range(2):
        g_re = filters[2 * p : 2 * p + 1, :] * scale
        g_im = filters[2 * p + 1 : 2 * p + 2, :] * scale
        x = raw[:, p * half : p * half + quarter]
        y = raw[:, p * half + quarter : (p + 1) * half]
        filtered = jnp.concatenate([g_re * x - g_im * y, g_re * y + g_im * x], axis=1)
        parts.append(jnp.dot(filtered.astype(BF16), tables[p], preferred_element_type=F32))
    early = (parts[0] + parts[1]).astype(BF16)
    late = (parts[0] - parts[1]).astype(BF16)
    for s in range(out.shape[0]):
        out[s, :, :half] = early[2 * s : 2 * s + 2]
        out[s, :, half:] = late[2 * s : 2 * s + 2]


def call(kernel, out_shape, kinds, out_kinds=None, scratch=(), limit=24):
    spaces = {"s": pltpu.SMEM, "v": pltpu.VMEM}
    many = isinstance(out_shape, (list, tuple))
    vmem = pl.BlockSpec(memory_space=pltpu.VMEM)
    return pl.pallas_call(
        kernel,
        out_shape=out_shape,
        in_specs=[pl.BlockSpec(memory_space=spaces[k]) for k in kinds],
        out_specs=[vmem] * len(out_shape) if many else vmem,
        scratch_shapes=list(scratch),
        compiler_params=pltpu.CompilerParams(vmem_limit_bytes=limit << 20),
    )


def per_device(ring_size, source_traces, surface_filter, records, owners, aperture):
    sources, own_traces, samples = source_traces.shape
    out_dev, aper = aperture.shape
    rec_dev = records.shape[0]
    half, quarter = samples // 2, samples // 4
    struct = jax.ShapeDtypeStruct
    where = jnp.stack([lax.axis_index("rx"), lax.axis_index("xl")]).astype(I32)
    swap = [(0, 1), (1, 0)]

    ringed = ring_size == 8 and own_traces == ROWS
    if ringed:
        order = [0, 2, 4, 6, 7, 5, 3, 1]
        up = [(order[i], order[(i + 1) % 8]) for i in range(8)]
        down = [(b, a) for a, b in up]
        steps = []
        a = b = source_traces
        for _ in range(3):
            a, b = lax.ppermute(a, "rx", up), lax.ppermute(b, "rx", down)
            steps.append((a, b))
        cut = sources // 2
        last = (lax.ppermute(a[:cut], "rx", up), lax.ppermute(b[cut:], "rx", down))

    other = lax.ppermute(records, "xl", swap)
    note = jnp.concatenate([owners.reshape(-1, aper), aperture], axis=0)
    noted = lax.ppermute(note, "xl", swap)
    core = where[1]
    pairs = rec_dev // aper
    entries = jnp.where(
        core == 0,
        jnp.concatenate([note[pairs:], noted[pairs:]], axis=0),
        jnp.concatenate([noted[pairs:], note[pairs:]], axis=0),
    )
    tags = jnp.concatenate(
        [
            note[:pairs].reshape(1, rec_dev),
            noted[:pairs].reshape(1, rec_dev),
            jnp.pad(entries, ((0, 0), (0, rec_dev - aper))),
        ],
        axis=0,
    )

    coarse, fine, inverse_coarse, inverse_fine = small_tables(samples)
    tables = call(forward_tables_kernel, struct((2, half, half), BF16), "vv")(coarse, fine)
    inverse = call(inverse_tables_kernel, struct((2, half, half), BF16), "vv")(
        inverse_coarse, inverse_fine
    )
    outs = 2 * out_dev
    chunks = aper // ROWS
    spectra = call(
        functools.partial(records_kernel, own_traces, aper),
        struct((outs, chunks, ROWS, samples), F32),
        "svvvv",
        limit=40,
    )(where, records, other, tags, tables)

    total_shape = struct((sources, outs, 8, samples), F32)

    def add(pieces, offsets, total):
        kernel = functools.partial(products_kernel, offsets, ringed, total is not None)
        arguments = [where, *pieces, tables, spectra] + ([] if total is None else [total])
        return call(
            kernel,
            [total_shape],
            "s" + "v" * (len(arguments) - 1),
            scratch=[pltpu.VMEM((len(pieces) * sources * ROWS, samples), F32)],
        )(*arguments)[0]

    if ringed:
        total = add([source_traces], [0], None)
        for k, (a, b) in enumerate(steps):
            total = add([a, b], [-(k + 1), k + 1], total)
        total = add([jnp.concatenate(last, axis=0)], [4], total)
    else:
        gathered = lax.all_gather(source_traces, "rx", axis=1, tiled=True)
        parts = [gathered[:, k * ROWS : (k + 1) * ROWS] for k in range(chunks)]
        total = None
        for k in range(0, chunks, 2):
            total = add(parts[k : k + 2], [k, k + 1], total)

    row_shape = struct((sources * out_dev, samples), F32)
    mine, theirs = call(reduce_kernel, [row_shape, row_shape], "sv")(where, total)
    arrived = lax.ppermute(theirs, "xl", swap)
    filters = surface_filter.reshape(2, quarter, 2).transpose(2, 0, 1).reshape(4, quarter)
    return call(
        functools.partial(finish_kernel, 1.0 / math.sqrt(aper)),
        struct((sources, out_dev, samples), BF16),
        "vvvv",
    )(filters, mine, arrived, inverse)


def solution(mesh):
    in_specs = (
        P(None, ("groups", "rx", "xl"), None),
        P(),
        P(("groups", "rx", "xl"), None),
        P(("groups", "rx", "xl")),
        P(("groups", "rx", "xl"), None),
    )
    out_specs = P(None, ("groups", "rx", "xl"), None)
    return jax.shard_map(
        functools.partial(per_device, mesh.shape["rx"]),
        mesh=mesh,
        in_specs=in_specs,
        out_specs=out_specs,
        check_vma=False,
    )
```

```python
import functools
import math

import jax
import jax.numpy as jnp
from jax import lax
from jax.experimental import pallas as pl
from jax.experimental.pallas import tpu as pltpu
from jax.sharding import PartitionSpec as P


F32, BF16, I32 = jnp.float32, jnp.bfloat16, jnp.int32
ROWS = 16
FORWARD_STEP = 32
INVERSE_STEP = 16


def turn(a, b):
    return a[0] * b[0] - a[1] * b[1], a[1] * b[0] + a[0] * b[1]


def angles(multiples, waves, samples):
    phase = ((multiples * waves) & (samples - 1)).astype(F32) * (2.0 * math.pi / samples)
    return jnp.cos(phase), jnp.sin(phase)


def row_of(pair, k):
    return pair[0][k : k + 1], pair[1][k : k + 1]


def build_forward(even, odd, fine):
    quarter = odd.shape[0]
    eighth = quarter // 2
    samples = 4 * quarter
    scale = 1.0 / math.sqrt(samples)
    first, ahead = [], []
    for k, rest in enumerate((0, 2, 1, 1)):
        row = lax.broadcasted_iota(I32, (8, eighth), 0)
        lane = lax.broadcasted_iota(I32, (8, eighth), 1)
        wave = 4 * (lane + (eighth if k == 3 else 0)) + rest
        columns = slice(k * eighth, (k + 1) * eighth)
        base = angles(row, wave, samples)
        jumps = angles(jnp.left_shift(8, jnp.minimum(row, 2)), wave, samples)
        base = (base[0] * scale, base[1] * scale)
        fine[0, 0:8, columns], fine[1, 0:8, columns] = base
        more = turn(base, row_of(jumps, 0))
        fine[0, 8:16, columns], fine[1, 8:16, columns] = more
        jump = row_of(jumps, 1)
        fine[0, 16:24, columns], fine[1, 16:24, columns] = turn(base, jump)
        fine[0, 24:32, columns], fine[1, 24:32, columns] = turn(more, jump)
        ahead.append(row_of(jumps, 2))
        first.append((jnp.ones((1, eighth), F32), jnp.zeros((1, eighth), F32)))

    def step(i, coarse):
        rows = pl.ds(i * FORWARD_STEP, FORWARD_STEP)
        for k in range(4):
            columns = slice(k * eighth, (k + 1) * eighth)
            cosine, sine = turn((fine[0, :, columns], fine[1, :, columns]), coarse[k])
            if k < 2:
                even[k, rows, :eighth] = cosine.astype(BF16)
                even[k, rows, eighth:] = (-sine).astype(BF16)
            else:
                start = (k - 2) * eighth
                odd[rows, start : start + eighth] = cosine.astype(BF16)
                odd[rows, quarter + start : quarter + start + eighth] = sine.astype(BF16)
        return [turn(a, b) for a, b in zip(coarse, ahead)]

    lax.fori_loop(0, quarter // FORWARD_STEP, step, first)


def forward_kernel(even, odd, fine):
    build_forward(even, odd, fine)


def inverse_kernel(even, odd, fine):
    quarter = odd.shape[0]
    eighth = quarter // 2
    samples = 4 * quarter
    scale = 1.0 / math.sqrt(samples // 2)
    row = lax.broadcasted_iota(I32, (8, quarter), 0)
    time = lax.broadcasted_iota(I32, (8, quarter), 1)
    base = angles(4 * row, time, samples)
    jumps = angles(jnp.where(row == 0, 32, jnp.where(row == 1, 64, row - 1)), time, samples)
    base = (base[0] * scale, base[1] * scale)
    base = (base, turn(base, row_of(jumps, 0)))
    for k, rest in enumerate((0, 2, 1)):
        for half in range(2):
            value = turn(base[half], row_of(jumps, 1 + rest)) if rest else base[half]
            rows = slice(8 * half, 8 * half + 8)
            fine[0, k, rows, :], fine[1, k, rows, :] = value
    ahead = row_of(jumps, 1)
    sign = 1.0 - 2.0 * (time[:1] & 1).astype(F32)

    def step(i, coarse):
        rows = pl.ds(i * INVERSE_STEP, INVERSE_STEP)
        later = pl.ds(eighth + i * INVERSE_STEP, INVERSE_STEP)
        for k in range(3):
            cosine, sine = turn((fine[0, k], fine[1, k]), coarse)
            if k < 2:
                even[k, rows, :] = cosine.astype(BF16)
                even[k, later, :] = (-sine).astype(BF16)
            else:
                odd[rows, :quarter] = cosine.astype(BF16)
                odd[rows, quarter:] = sine.astype(BF16)
                odd[later, :quarter] = (cosine * sign).astype(BF16)
                odd[later, quarter:] = (sine * sign).astype(BF16)
        return turn(coarse, ahead)

    first = (jnp.ones((1, quarter), F32), jnp.zeros((1, quarter), F32))
    lax.fori_loop(0, eighth // INVERSE_STEP, step, first)


def filters_kernel(filters, out):
    count = filters.shape[1]
    part = count // 4
    column = lax.broadcasted_iota(I32, (count, count), 1)
    source = jnp.where(
        column < 2 * part,
        jnp.where(column < part, 4 * column, 4 * (column - part) + 2),
        jnp.where(column < 3 * part, 4 * (column - 2 * part) + 1, 4 * (count - 1 - column) + 3),
    )
    move = (lax.broadcasted_iota(I32, (count, count), 0) == source).astype(F32).astype(BF16)
    left = filters[...]
    moved = jnp.zeros((2, count), F32)
    for _ in range(3):
        piece = left.astype(BF16)
        left = left - piece.astype(F32)
        moved = moved + jnp.dot(piece, move, preferred_element_type=F32)
    column = lax.broadcasted_iota(I32, (1, count), 1)
    out[0:1, :] = moved[0:1]
    out[1:2, :] = jnp.where(column < 3 * part, moved[1:2], -moved[1:2])


def split(x):
    quarter = x.shape[-1] // 4
    x0, x1, x2, x3 = (x[:, q * quarter : (q + 1) * quarter].astype(F32) for q in range(4))
    first, second = x0 + x2, x1 + x3
    return (
        (first + second).astype(BF16),
        (first - second).astype(BF16),
        (x0 - x2).astype(BF16),
        (x3 - x1).astype(BF16),
    )


def transform(parts, even, odd):
    rows = parts[0].shape[0]
    quarter = odd.shape[0]
    dot = functools.partial(jnp.dot, preferred_element_type=F32)
    both = dot(jnp.concatenate(parts[2:], axis=0), odd[...])
    return (
        dot(parts[0], even[0]),
        dot(parts[1], even[1]),
        both[:rows, :quarter] + both[rows:, quarter:],
        both[rows:, :quarter] - both[:rows, quarter:],
    )


def groups(samples):
    quarter, eighth = samples // 4, samples // 8
    return ((0, eighth, eighth), (quarter, eighth, eighth), (2 * quarter, quarter, quarter))


def setup_kernel(per_device, aper, place, *refs):
    sources, out = refs[:6], refs[6]
    data, owners, owners_other, entries, entries_other = refs[7:12]
    even, odd, fine, result, arriving, leaving = refs[12:]
    rec_dev, samples = sources[0].shape
    targets = (data.at[:rec_dev], data.at[rec_dev:], owners, owners_other, entries, entries_other)
    copies = [
        pltpu.make_async_copy(source, target, arriving.at[k])
        for k, (source, target) in enumerate(zip(sources, targets))
    ]
    for copy in copies:
        copy.start()
    build_forward(even, odd, fine)
    core = place[0]
    for copy in copies[2:]:
        copy.wait()
    slots = 2 * rec_dev
    outs = slots // aper
    out_dev = outs // 2
    earlier = (
        lax.broadcasted_iota(I32, (rec_dev, rec_dev), 0)
        < lax.broadcasted_iota(I32, (rec_dev, rec_dev), 1)
    ).astype(F32).astype(BF16)
    sides = (owners[...], owners_other[...])
    ranks, totals = [], []
    for owner in sides:
        mine = (owner == core).astype(F32)
        rank = jnp.dot(
            jnp.broadcast_to(mine, (8, rec_dev)).astype(BF16), earlier, preferred_element_type=F32
        )
        ranks.append(rank[:1])
        totals.append(jnp.sum(mine, axis=1, keepdims=True))
    position = lax.broadcasted_iota(I32, (1, rec_dev), 1)
    slot_row = lax.broadcasted_iota(I32, (slots, rec_dev), 0)
    picks = []
    for side in range(2):
        second = core != side
        before = (ranks[side] + jnp.where(second, totals[1 - side], 0.0)).astype(I32)
        index = position + jnp.where(second, rec_dev, 0)
        slot = jnp.where(sides[side] == core, before, rec_dev + index - before)
        picks.append((slot_row == slot).astype(F32).astype(BF16))
    picks = jnp.concatenate(picks, axis=1)
    trace = lax.broadcasted_iota(I32, (aper, aper), 0)
    trace = trace // per_device * (2 * per_device) + core * per_device + trace % per_device
    rows = []
    for r in range(outs):
        row = slice(r % out_dev, r % out_dev + 1)
        entry = (entries if r < out_dev else entries_other)[row, :]
        match = (trace == entry).astype(F32).astype(BF16)
        pick = picks[r * aper : (r + 1) * aper]
        rows.append(jnp.dot(match, pick, preferred_element_type=F32).astype(BF16))
    placed = jnp.concatenate(rows, axis=0)
    for copy in copies[:2]:
        copy.wait()
    routed = jnp.dot(placed, data[...], preferred_element_type=F32)
    first, sent = 0, []
    for k, block in enumerate(transform(split(routed), even, odd)):
        columns = slice(first, first + block.shape[1])
        first += block.shape[1]
        block = block.reshape(outs, aper // ROWS, ROWS, block.shape[1])
        for r in range(outs):
            result[:, r, :, columns] = block[r]
        copy = pltpu.make_async_copy(
            result.at[:, :, :, columns], out.at[:, :, :, columns], leaving.at[k]
        )
        copy.start()
        sent.append(copy)
    for copy in sent:
        copy.wait()


def ring_chunk(me, offset):
    place = jnp.where(me % 2 == 0, me // 2, 7 - me // 2)
    place = (place + offset) % 8
    return jnp.where(place < 4, 2 * place, 15 - 2 * place)


def sum_rows(values):
    row = lax.broadcasted_iota(I32, values[0].shape, 0)
    for shift in (4, 2, 1):
        upper = row % (2 * shift) < shift
        half = len(values) // 2
        joined = []
        for a, b in zip(values[:half], values[half:]):
            if shift == 4:
                rolled = pltpu.roll(jnp.where(upper, b, a), 4, 0)
            else:
                rolled = jnp.where(upper, pltpu.roll(a, 8 - shift, 0), pltpu.roll(b, shift, 0))
            joined.append(jnp.where(upper, a, b) + rolled)
        values = joined
    return values[0]


def halves_kernel(*refs):
    values, outs = refs[: len(refs) // 3], refs[len(refs) // 3 :]
    cut = outs[0].shape[0]
    for k, value in enumerate(values):
        outs[2 * k][...] = value[:cut]
        outs[2 * k + 1][...] = value[cut:]


def products_kernel(offsets, count, ringed, with_total, extra, place, *refs):
    pieces = refs[:count]
    even, odd, spectra = refs[count : count + 3]
    totals = refs[count + 3 : count + 3 + 2 * with_total]
    outs = refs[count + 3 + 2 * with_total + extra : -3]
    work, right, arriving = refs[-3:]
    copies = []
    for c, offset in enumerate(offsets):
        chunk = ring_chunk(place[0], offset) if ringed else offset
        copies.append(pltpu.make_async_copy(spectra.at[chunk], right.at[c], arriving.at[c]))
        copies[-1].start()
    samples = work.shape[1]
    number = right.shape[1]
    rows = work.shape[0] // len(offsets)
    sources = rows // ROWS
    data = jnp.concatenate([x[...].reshape(-1, samples) for x in pieces], axis=0)
    first = 0
    for block in transform(split(data), even, odd):
        work[:, first : first + block.shape[1]] = block
        first += block.shape[1]
    for copy in copies:
        copy.wait()
    if len(outs) > 2:
        outs[2][...] = jnp.zeros(outs[2].shape, F32)
    for start, distance, width in groups(samples):
        for block in range(width // 128):
            re = pl.ds(start + block * 128, 128)
            im = pl.ds(start + distance + block * 128, 128)
            sums = {}
            for c in range(len(offsets)):
                for r in range(number):
                    for h in range(ROWS // 8):
                        b_re, b_im = (right[c, r, 8 * h : 8 * h + 8, k] for k in (re, im))
                        for s in range(sources):
                            top = c * rows + s * ROWS + h * 8
                            a_re, a_im = work[top : top + 8, re], work[top : top + 8, im]
                            x = a_re * b_re - a_im * b_im
                            y = a_re * b_im + a_im * b_re
                            if (s, r) in sums:
                                x, y = x + sums[s, r][0], y + sums[s, r][1]
                            sums[s, r] = (x, y)
            share = number // 2
            for i in range(2):
                keys = [(s, i * share + r) for r in range(share) for s in range(sources)]
                for part, columns in enumerate((re, im)):
                    value = sum_rows([sums[key][part] for key in keys])
                    if with_total:
                        value = value + totals[i][:, columns]
                    outs[i][:, columns] = value


def finish_kernel(scale, filters, mine, arrived, even, odd, out):
    quarter = odd.shape[0]
    sources, out_dev, samples = out.shape
    raw = mine[...] + arrived[...]
    dot = functools.partial(jnp.dot, preferred_element_type=F32)
    filtered = []
    column = 0
    for start, distance, width in groups(samples):
        g_re = filters[0:1, column : column + width] * scale
        g_im = filters[1:2, column : column + width] * scale
        column += width
        x = raw[:, start : start + width]
        y = raw[:, start + distance : start + distance + width]
        filtered.append((g_re * x - g_im * y, g_re * y + g_im * x))
    a = dot(jnp.concatenate(filtered[0], axis=1).astype(BF16), even[0])
    b = dot(jnp.concatenate(filtered[1], axis=1).astype(BF16), even[1])
    both = dot(jnp.concatenate(filtered[2], axis=0).astype(BF16), odd[...])
    rows = raw.shape[0]
    h_re = both[:rows, :quarter] - both[rows:, quarter:]
    h_im = both[:rows, quarter:] + both[rows:, :quarter]
    plus, minus = a + b, a - b
    for q, value in enumerate((plus + h_re, minus - h_im, plus - h_re, minus + h_im)):
        value = value.reshape(out_dev, sources, quarter)
        for r in range(out_dev):
            out[:, r, q * quarter : (q + 1) * quarter] = value[r].astype(BF16)


def call(kernel, out_shape, kinds, scratch=(), limit=48, out_kinds=None):
    spaces = {"s": pltpu.SMEM, "v": pltpu.VMEM, "a": pl.ANY}
    specs = [pl.BlockSpec(memory_space=spaces[k]) for k in kinds]
    return pl.pallas_call(
        kernel,
        out_shape=out_shape,
        in_specs=specs,
        out_specs=[
            pl.BlockSpec(memory_space=spaces[k]) for k in out_kinds or "v" * len(out_shape)
        ],
        scratch_shapes=list(scratch),
        compiler_params=pltpu.CompilerParams(vmem_limit_bytes=limit << 20),
    )


def per_device(ring_size, source_traces, surface_filter, records, owners, aperture):
    sources, own_traces, samples = source_traces.shape
    out_dev, aper = aperture.shape
    rec_dev = records.shape[0]
    quarter = samples // 4
    struct = jax.ShapeDtypeStruct
    rx, xl = (lax.axis_index(axis).astype(I32).reshape(1) for axis in ("rx", "xl"))
    outs = 2 * out_dev
    chunks = aper // ROWS
    token = struct((8, 128), F32)

    def after(token, *values):
        return lax.optimization_barrier((*values, token))

    def swap(x):
        return lax.ppermute(x, "xl", [(0, 1), (1, 0)])

    owners = owners.reshape(1, -1)
    table_shapes = [struct((2, quarter, quarter), BF16), struct((quarter, 2 * quarter), BF16)]
    table_scratch = pltpu.VMEM((2, FORWARD_STEP, 2 * quarter), F32)

    def setup():
        spectra_shape = (chunks, outs, ROWS, samples)
        return call(
            functools.partial(setup_kernel, own_traces, aper),
            [struct(spectra_shape, F32)],
            "s" + "a" * 6,
            [
                pltpu.VMEM((2 * rec_dev, samples), BF16),
                *[pltpu.VMEM((1, rec_dev), I32)] * 2,
                *[pltpu.VMEM((out_dev, aper), I32)] * 2,
                *[pltpu.VMEM(shape.shape, BF16) for shape in table_shapes],
                table_scratch,
                pltpu.VMEM(spectra_shape, F32),
                pltpu.SemaphoreType.DMA((6,)),
                pltpu.SemaphoreType.DMA((4,)),
            ],
            61,
            "a",
        )(xl, records, swap(records), owners, swap(owners), aperture, swap(aperture))[0]

    def arrange(filters):
        return call(filters_kernel, [struct(filters.shape, F32)], "v")(filters)[0]

    def add(pieces, offsets, totals, ringed, extra=()):
        kernel = functools.partial(
            products_kernel, offsets, len(pieces), ringed, bool(totals), len(extra)
        )
        arguments = [*pieces, *tables, spectra, *totals, *extra]
        row_shape = struct((out_dev * sources, samples), F32)
        kinds = "s" + "v" * (len(pieces) + 2) + "a" + "v" * (len(totals) + len(extra))
        count = len(offsets)
        *result, done = call(
            kernel,
            [row_shape, row_shape, token],
            kinds,
            [
                pltpu.VMEM((count * sources * ROWS, samples), F32),
                pltpu.VMEM((count, outs, ROWS, samples), F32),
                pltpu.SemaphoreType.DMA((count,)),
            ],
        )(rx, *arguments)
        return result, done

    if ring_size == 8 and own_traces == ROWS:
        order = [0, 2, 4, 6, 7, 5, 3, 1]
        up = [(order[i], order[(i + 1) % 8]) for i in range(8)]
        down = [(b, a) for a, b in up]

        def step(a, b):
            return lax.ppermute(a, "rx", up), lax.ppermute(b, "rx", down)

        a1, b1 = step(source_traces, source_traces)
        *held, spectra = after(setup(), a1, b1)
        a2, b2 = step(*held)
        tables = call(forward_kernel, table_shapes, "", [table_scratch])()
        pieces = [source_traces, a1, b1]
        totals, done = add(pieces, [0, -1, 1], [], True)
        a2, b2, done = after(done, a2, b2)
        half = struct((sources // 2, own_traces, samples), BF16)
        up_first, up_second, down_first, down_second = call(halves_kernel, [half] * 4, "vv")(a2, b2)
        up_first, down_second = step(up_first, down_second)
        up_second, down_first = step(up_second, down_first)
        pieces = [up_first, up_second, down_first, down_second]
        totals, done = add([a2, b2], [-2, 2], totals, True, [done])
        up_first, down_second, surface_filter, done = after(
            done, up_first, down_second, surface_filter
        )
        last = step(up_first, down_second)
        filters = arrange(surface_filter)
        totals, _ = add(pieces, [-3, 3], totals, True, [done])
        (mine, theirs), _ = add(last, [4], totals, True)
    else:
        spectra = setup()
        tables = call(forward_kernel, table_shapes, "", [table_scratch])()
        gathered = lax.all_gather(source_traces, "rx", axis=1, tiled=True)
        parts = [gathered[:, k * ROWS : (k + 1) * ROWS] for k in range(chunks)]
        totals = []
        for k in range(0, chunks, 2):
            totals, _ = add(parts[k : k + 2], [k, k + 1], totals, False)
        mine, theirs = totals
        filters = arrange(surface_filter)

    fine = pltpu.VMEM((2, 3, INVERSE_STEP, quarter), F32)
    inverse = call(inverse_kernel, table_shapes, "", [fine])()
    return call(
        functools.partial(finish_kernel, 1.0 / math.sqrt(aper)),
        [struct((sources, out_dev, samples), BF16)],
        "vvvvv",
    )(filters, mine, swap(theirs), *inverse)[0]


def solution(mesh):
    in_specs = (
        P(None, ("groups", "rx", "xl"), None),
        P(),
        P(("groups", "rx", "xl"), None),
        P(("groups", "rx", "xl")),
        P(("groups", "rx", "xl"), None),
    )
    out_specs = P(None, ("groups", "rx", "xl"), None)
    return jax.shard_map(
        functools.partial(per_device, mesh.shape["rx"]),
        mesh=mesh,
        in_specs=in_specs,
        out_specs=out_specs,
        check_vma=False,
    )
```

```python
import functools
import math

import jax
import jax.numpy as jnp
from jax import lax
from jax.experimental import pallas as pl
from jax.experimental.pallas import tpu as pltpu
from jax.sharding import PartitionSpec as P


F32, BF16, I32 = jnp.float32, jnp.bfloat16, jnp.int32
ROWS = 16
FORWARD_STEP = 32
INVERSE_STEP = 16


def turn(a, b):
    return a[0] * b[0] - a[1] * b[1], a[1] * b[0] + a[0] * b[1]


def angles(multiples, waves, samples):
    phase = ((multiples * waves) & (samples - 1)).astype(F32) * (2.0 * math.pi / samples)
    return jnp.cos(phase), jnp.sin(phase)


def row_of(pair, k):
    return pair[0][k : k + 1], pair[1][k : k + 1]


def build_forward(even, odd, fine):
    count = even.shape[1]
    part = count // 2
    samples = 8 * count
    scale = 1.0 / math.sqrt(samples)
    first, ahead = [], []
    for k, rest in enumerate((0, 2, 1, 5)):
        row = lax.broadcasted_iota(I32, (8, count), 0)
        lane = lax.broadcasted_iota(I32, (8, count), 1)
        wave = 8 * lane + rest
        if k == 0:
            wave = jnp.where(lane < part, 8 * lane, 8 * (lane - part) + 4)
        columns = slice(k * count, (k + 1) * count)
        base = angles(row, wave, samples)
        jumps = angles(jnp.left_shift(8, jnp.minimum(row, 2)), wave, samples)
        base = (base[0] * scale, base[1] * scale)
        fine[0, 0:8, columns], fine[1, 0:8, columns] = base
        more = turn(base, row_of(jumps, 0))
        fine[0, 8:16, columns], fine[1, 8:16, columns] = more
        jump = row_of(jumps, 1)
        fine[0, 16:24, columns], fine[1, 16:24, columns] = turn(base, jump)
        fine[0, 24:32, columns], fine[1, 24:32, columns] = turn(more, jump)
        ahead.append(row_of(jumps, 2))
        first.append((jnp.ones((1, count), F32), jnp.zeros((1, count), F32)))

    def step(i, coarse):
        rows = pl.ds(i * FORWARD_STEP, FORWARD_STEP)
        for k in range(4):
            columns = slice(k * count, (k + 1) * count)
            cosine, sine = turn((fine[0, :, columns], fine[1, :, columns]), coarse[k])
            if k == 0:
                for g in range(2):
                    even[g, rows, :part] = cosine[:, g * part : (g + 1) * part].astype(BF16)
                    even[g, rows, part:] = (-sine[:, g * part : (g + 1) * part]).astype(BF16)
            else:
                odd[k - 1, rows, :count] = cosine.astype(BF16)
                odd[k - 1, rows, count:] = sine.astype(BF16)
        return [turn(a, b) for a, b in zip(coarse, ahead)]

    lax.fori_loop(0, count // FORWARD_STEP, step, first)


def forward_kernel(rx, xl, even, odd, fine):
    build_forward(even, odd, fine)


def inverse_kernel(even, odd, fine):
    count = even.shape[1]
    part = count // 2
    samples = 8 * count
    scale = 1.0 / math.sqrt(samples // 2)
    row = lax.broadcasted_iota(I32, (8, count), 0)
    time = lax.broadcasted_iota(I32, (8, count), 1)
    base = angles(8 * row, time, samples)
    jumps = angles(jnp.where(row == 0, 64, jnp.where(row == 1, 128, row - 1)), time, samples)
    base = (base[0] * scale, base[1] * scale)
    base = (base, turn(base, row_of(jumps, 0)))
    for k, rest in enumerate((0, 4, 2, 1, 5)):
        for half in range(2):
            value = turn(base[half], row_of(jumps, 1 + rest)) if rest else base[half]
            rows = slice(8 * half, 8 * half + 8)
            fine[0, k, rows, :], fine[1, k, rows, :] = value
    ahead = row_of(jumps, 1)
    sign = 1.0 - 2.0 * (time[:1] & 1).astype(F32)

    def step(i, coarse):
        rows = pl.ds(i * INVERSE_STEP, INVERSE_STEP)
        later = pl.ds(part + i * INVERSE_STEP, INVERSE_STEP)
        for k in range(5):
            cosine, sine = turn((fine[0, k], fine[1, k]), coarse)
            if k < 2:
                even[k, rows, :] = cosine.astype(BF16)
                even[k, later, :] = (-sine).astype(BF16)
            else:
                odd[k - 2, rows, :count] = cosine.astype(BF16)
                odd[k - 2, rows, count:] = sine.astype(BF16)
                odd[k - 2, later, :count] = (cosine * sign).astype(BF16)
                odd[k - 2, later, count:] = (sine * sign).astype(BF16)
        return turn(coarse, ahead)

    first = (jnp.ones((1, count), F32), jnp.zeros((1, count), F32))
    lax.fori_loop(0, part // INVERSE_STEP, step, first)


def filters_kernel(filters, out):
    count = filters.shape[1]
    part = count // 8
    column = lax.broadcasted_iota(I32, (count, count), 1)
    block, inner = column // part, column % part
    rest = jnp.zeros_like(column)
    for k, value in enumerate((0, 4, 2, 6, 1, 7, 5, 3)):
        rest = jnp.where(block == k, value, rest)
    upper = ((block == 3) | (block == 5) | (block == 7)).astype(I32)
    source = 8 * jnp.where(upper == 1, part - 1 - inner, inner) + rest
    move = (lax.broadcasted_iota(I32, (count, count), 0) == source).astype(F32).astype(BF16)
    left = filters[...]
    moved = jnp.zeros((2, count), F32)
    for _ in range(3):
        piece = left.astype(BF16)
        left = left - piece.astype(F32)
        moved = moved + jnp.dot(piece, move, preferred_element_type=F32)
    out[0:1, :] = moved[0:1]
    out[1:2, :] = jnp.where(upper[:1] == 1, -moved[1:2], moved[1:2])


def split(x):
    quarter = x.shape[-1] // 4
    half = quarter // 2
    x0, x1, x2, x3 = (x[:, q * quarter : (q + 1) * quarter].astype(F32) for q in range(4))
    first, second = x0 + x2, x1 + x3
    p, q = first + second, first - second
    re, im = x0 - x2, x3 - x1
    root = math.sqrt(0.5)
    turned_re = root * (re[:, half:] + im[:, half:])
    turned_im = root * (im[:, half:] - re[:, half:])
    re, im = re[:, :half], im[:, :half]
    return (
        (p[:, :half] + p[:, half:]).astype(BF16),
        (p[:, :half] - p[:, half:]).astype(BF16),
        (q[:, :half].astype(BF16), (-q[:, half:]).astype(BF16)),
        ((re + turned_re).astype(BF16), (im + turned_im).astype(BF16)),
        ((re - turned_re).astype(BF16), (im - turned_im).astype(BF16)),
    )


def transform(parts, even, odd):
    rows = parts[0].shape[0]
    count = even.shape[1]
    dot = functools.partial(jnp.dot, preferred_element_type=F32)
    for g in range(2):
        yield dot(parts[g], even[g])
    for g in range(3):
        both = dot(jnp.concatenate(parts[2 + g], axis=0), odd[g])
        yield both[:rows, :count] + both[rows:, count:]
        yield both[rows:, :count] - both[:rows, count:]


def groups(samples):
    count = samples // 8
    part = count // 2
    full = [(2 * count + 2 * g * count, count, count) for g in range(3)]
    return [(0, part, part), (count, part, part), *full]


def setup_kernel(per_device, aper, place, own, other, notes, notes_other, even, odd, out, token, data, arriving):
    rec_dev, samples = own.shape
    copies = [
        pltpu.make_async_copy(source, data.at[k * rec_dev : (k + 1) * rec_dev], arriving.at[k])
        for k, source in enumerate((own, other))
    ]
    for copy in copies:
        copy.start()
    core = place[0]
    slots = 2 * rec_dev
    outs = slots // aper
    out_dev = outs // 2
    earlier = (
        lax.broadcasted_iota(I32, (rec_dev, rec_dev), 0)
        < lax.broadcasted_iota(I32, (rec_dev, rec_dev), 1)
    ).astype(F32).astype(BF16)
    lines = rec_dev // aper
    sides = [
        jnp.concatenate([note[k : k + 1, :] for k in range(lines)], axis=1)
        for note in (notes, notes_other)
    ]
    ranks, totals = [], []
    for owner in sides:
        mine = (owner == core).astype(F32)
        rank = jnp.dot(
            jnp.broadcast_to(mine, (8, rec_dev)).astype(BF16), earlier, preferred_element_type=F32
        )
        ranks.append(rank[:1])
        totals.append(jnp.sum(mine, axis=1, keepdims=True))
    position = lax.broadcasted_iota(I32, (1, rec_dev), 1)
    slot_row = lax.broadcasted_iota(I32, (slots, rec_dev), 0)
    picks = []
    for side in range(2):
        second = core != side
        before = (ranks[side] + jnp.where(second, totals[1 - side], 0.0)).astype(I32)
        index = position + jnp.where(second, rec_dev, 0)
        slot = jnp.where(sides[side] == core, before, rec_dev + index - before)
        picks.append((slot_row == slot).astype(F32).astype(BF16))
    picks = jnp.concatenate(picks, axis=1)
    trace = lax.broadcasted_iota(I32, (aper, aper), 0)
    trace = trace // per_device * (2 * per_device) + core * per_device + trace % per_device
    rows = []
    for r in range(outs):
        line = lines + r % out_dev
        entry = (notes if r < out_dev else notes_other)[line : line + 1, :]
        match = (trace == entry).astype(F32).astype(BF16)
        pick = picks[r * aper : (r + 1) * aper]
        rows.append(jnp.dot(match, pick, preferred_element_type=F32).astype(BF16))
    placed = jnp.concatenate(rows, axis=0)
    for copy in copies:
        copy.wait()
    routed = jnp.dot(placed, data[...], preferred_element_type=F32)
    first = 0
    for block in transform(split(routed), even, odd):
        width = block.shape[1]
        block = block.astype(BF16).reshape(outs, aper // ROWS, ROWS, width)
        for r in range(outs):
            out[:, r, :, first : first + width] = block[r]
        first += width
    token[...] = jnp.zeros(token.shape, F32)


def ring_chunk(me, offset):
    place = jnp.where(me % 2 == 0, me // 2, 7 - me // 2)
    place = (place + offset) % 8
    return jnp.where(place < 4, 2 * place, 15 - 2 * place)


def sum_rows(values):
    row = lax.broadcasted_iota(I32, values[0].shape, 0)
    for shift in (4, 2, 1):
        upper = row % (2 * shift) < shift
        half = len(values) // 2
        joined = []
        for a, b in zip(values[:half], values[half:]):
            if shift == 4:
                rolled = pltpu.roll(jnp.where(upper, b, a), 4, 0)
            else:
                rolled = jnp.where(upper, pltpu.roll(a, 8 - shift, 0), pltpu.roll(b, shift, 0))
            joined.append(jnp.where(upper, a, b) + rolled)
        values = joined
    return values[0]


def halves_kernel(*refs):
    values, outs = refs[: len(refs) // 3], refs[len(refs) // 3 :]
    cut = outs[0].shape[0]
    for k, value in enumerate(values):
        outs[2 * k][...] = value[:cut]
        outs[2 * k + 1][...] = value[cut:]


def products_kernel(offsets, count, ringed, with_total, extra, place, *refs):
    pieces = refs[:count]
    even, odd, spectra = refs[count : count + 3]
    totals = refs[count + 3 : count + 3 + 2 * with_total]
    outs = refs[count + 3 + 2 * with_total + extra : -1]
    work = refs[-1]
    chunks = [ring_chunk(place[0], offset) if ringed else offset for offset in offsets]
    samples = work.shape[1]
    number = spectra.shape[1]
    rows = work.shape[0] // len(offsets)
    sources = rows // ROWS
    data = jnp.concatenate([x[...].reshape(-1, samples) for x in pieces], axis=0)
    first = 0
    for block in transform(split(data), even, odd):
        work[:, first : first + block.shape[1]] = block
        first += block.shape[1]
    if len(outs) > 2:
        outs[2][...] = jnp.zeros(outs[2].shape, F32)
    for start, distance, width in groups(samples):
        for block in range(width // 128):
            re = pl.ds(start + block * 128, 128)
            im = pl.ds(start + distance + block * 128, 128)
            sums = {}
            for c in range(len(offsets)):
                for r in range(number):
                    right = [spectra[chunks[c], r, :, k].astype(F32) for k in (re, im)]
                    for h in range(ROWS // 8):
                        b_re, b_im = (b[8 * h : 8 * h + 8] for b in right)
                        for s in range(sources):
                            top = c * rows + s * ROWS + h * 8
                            a_re, a_im = work[top : top + 8, re], work[top : top + 8, im]
                            x = a_re * b_re - a_im * b_im
                            y = a_re * b_im + a_im * b_re
                            if (s, r) in sums:
                                x, y = x + sums[s, r][0], y + sums[s, r][1]
                            sums[s, r] = (x, y)
            share = number // 2
            for i in range(2):
                keys = [(s, i * share + r) for r in range(share) for s in range(sources)]
                for part, columns in enumerate((re, im)):
                    value = sum_rows([sums[key][part] for key in keys])
                    if with_total:
                        value = value + totals[i][:, columns]
                    outs[i][:, columns] = value


def finish_kernel(scale, filters, mine, arrived, even, odd, out):
    count = even.shape[1]
    sources, out_dev, samples = out.shape
    raw = mine[...] + arrived[...]
    rows = raw.shape[0]
    dot = functools.partial(jnp.dot, preferred_element_type=F32)
    waves, column = [], 0
    for g, (start, distance, width) in enumerate(groups(samples)):
        g_re = filters[0:1, column : column + width] * scale
        g_im = filters[1:2, column : column + width] * scale
        column += width
        x = raw[:, start : start + width]
        y = raw[:, start + distance : start + distance + width]
        x, y = g_re * x - g_im * y, g_re * y + g_im * x
        if g < 2:
            waves.append(dot(jnp.concatenate([x, y], axis=1).astype(BF16), even[g]))
        else:
            both = dot(jnp.concatenate([x, y], axis=0).astype(BF16), odd[g - 2])
            waves.append(both[:rows, :count] - both[rows:, count:])
            waves.append(both[:rows, count:] + both[rows:, :count])
    a, b, h_re, h_im, v_re, v_im, w_re, w_im = waves
    root = math.sqrt(0.5)
    plus, minus = a + b, a - b
    u_re, u_im = v_re + w_re, v_im + w_im
    v_re, v_im = v_re - w_re, v_im - w_im
    less, more = root * (v_re - v_im), root * (v_re + v_im)
    results = (
        plus + h_re + u_re,
        minus - h_im + less,
        plus - h_re - u_im,
        minus + h_im - more,
        plus + h_re - u_re,
        minus - h_im - less,
        plus - h_re + u_im,
        minus + h_im + more,
    )
    for k, value in enumerate(results):
        value = value.reshape(out_dev, sources, count)
        for r in range(out_dev):
            out[:, r, k * count : (k + 1) * count] = value[r].astype(BF16)


def call(kernel, out_shape, kinds, scratch=(), limit=24, cost=1):
    spaces = {"s": pltpu.SMEM, "v": pltpu.VMEM, "a": pl.ANY}
    specs = [pl.BlockSpec(memory_space=spaces[k]) for k in kinds]
    return pl.pallas_call(
        kernel,
        out_shape=out_shape,
        in_specs=specs,
        out_specs=[pl.BlockSpec(memory_space=pltpu.VMEM)] * len(out_shape),
        cost_estimate=pl.CostEstimate(
            flops=cost * 10**9, transcendentals=0, bytes_accessed=cost * 3 * 10**6
        ),
        scratch_shapes=list(scratch),
        compiler_params=pltpu.CompilerParams(vmem_limit_bytes=limit << 20),
    )


def per_device(ring_size, source_traces, surface_filter, records, owners, aperture):
    sources, own_traces, samples = source_traces.shape
    out_dev, aper = aperture.shape
    rec_dev = records.shape[0]
    count = samples // 8
    struct = jax.ShapeDtypeStruct
    rx, xl = (lax.axis_index(axis).astype(I32).reshape(1) for axis in ("rx", "xl"))
    outs = 2 * out_dev
    chunks = aper // ROWS
    token = struct((8, 128), F32)

    def after(token, *values):
        return lax.optimization_barrier((*values, token))

    def swap(x):
        return lax.ppermute(x, "xl", [(0, 1), (1, 0)])

    notes = jnp.concatenate([owners.reshape(-1, aper), aperture], axis=0)
    table_shapes = [struct((2, count, count), BF16), struct((3, count, 2 * count), BF16)]
    fine = [pltpu.VMEM((2, FORWARD_STEP, 4 * count), F32)]
    tables = call(forward_kernel, table_shapes, "ss", fine)(rx, xl)

    def setup():
        return call(
            functools.partial(setup_kernel, own_traces, aper),
            [struct((chunks, outs, ROWS, samples), BF16), token],
            "saavvvv",
            [pltpu.VMEM((2 * rec_dev, samples), BF16), pltpu.SemaphoreType.DMA((2,))],
            cost=4,
        )(xl, records, swap(records), notes, swap(notes), *tables)

    def arrange(filters):
        return call(filters_kernel, [struct(filters.shape, F32)], "v")(filters)[0]

    def add(pieces, offsets, totals, ringed, extra=()):
        kernel = functools.partial(
            products_kernel, offsets, len(pieces), ringed, bool(totals), len(extra)
        )
        arguments = [*pieces, *tables, spectra, *totals, *extra]
        row_shape = struct((out_dev * sources, samples), F32)
        kinds = "s" + "v" * len(arguments)
        *result, done = call(
            kernel,
            [row_shape, row_shape, token],
            kinds,
            [pltpu.VMEM((len(offsets) * sources * ROWS, samples), F32)],
        )(rx, *arguments)
        return result, done

    if ring_size == 8 and own_traces == ROWS:
        order = [0, 2, 4, 6, 7, 5, 3, 1]
        up = [(order[i], order[(i + 1) % 8]) for i in range(8)]
        down = [(b, a) for a, b in up]

        def rise(x):
            return lax.ppermute(x, "rx", up)

        def fall(x):
            return lax.ppermute(x, "rx", down)

        half = struct((sources // 2, own_traces, samples), BF16)

        def halves(x):
            return call(halves_kernel, [half] * 2, "v")(x)

        a1, b1 = rise(source_traces), fall(source_traces)
        spectra, done = setup()
        a2, first = after(done, a1)
        b2, second = after(done, b1)
        a2, b2 = rise(a2), fall(b2)
        totals, done = add([source_traces, a1, b1], [0, -1, 1], [], True, [first, second])
        filters = arrange(surface_filter)
        a3, filters, first = after(done, a2, filters)
        b3, second = after(done, b2)
        a3_sent, a3_kept = halves(a3)
        b3_kept, b3_sent = halves(b3)
        a3_sent, b3_sent = rise(a3_sent), fall(b3_sent)
        a3_kept, b3_kept = rise(a3_kept), fall(b3_kept)
        totals, done = add([a2, b2], [-2, 2], totals, True, [first, second])
        a4, first = after(done, a3_sent)
        b4, second = after(done, b3_sent)
        a4, b4 = rise(a4), fall(b4)
        pieces = [a3_sent, a3_kept, b3_kept, b3_sent]
        totals, _ = add(pieces, [-3, 3], totals, True, [first, second])
        (mine, theirs), _ = add([a4, b4], [4], totals, True)
    else:
        spectra, _ = setup()
        gathered = lax.all_gather(source_traces, "rx", axis=1, tiled=True)
        parts = [gathered[:, k * ROWS : (k + 1) * ROWS] for k in range(chunks)]
        totals = []
        for k in range(0, chunks, 2):
            totals, _ = add(parts[k : k + 2], [k, k + 1], totals, False)
        mine, theirs = totals
        filters = arrange(surface_filter)

    fine = [pltpu.VMEM((2, 5, INVERSE_STEP, count), F32)]
    inverse = call(inverse_kernel, table_shapes, "", fine)()
    return call(
        functools.partial(finish_kernel, 1.0 / math.sqrt(aper)),
        [struct((sources, out_dev, samples), BF16)],
        "vvvvv",
    )(filters, mine, swap(theirs), *inverse)[0]


def solution(mesh):
    in_specs = (
        P(None, ("groups", "rx", "xl"), None),
        P(),
        P(("groups", "rx", "xl"), None),
        P(("groups", "rx", "xl")),
        P(("groups", "rx", "xl"), None),
    )
    out_specs = P(None, ("groups", "rx", "xl"), None)
    return jax.shard_map(
        functools.partial(per_device, mesh.shape["rx"]),
        mesh=mesh,
        in_specs=in_specs,
        out_specs=out_specs,
        check_vma=False,
    )
```

```python
import functools
import math

import jax
import jax.numpy as jnp
from jax import lax
from jax.experimental import pallas as pl
from jax.experimental.pallas import tpu as pltpu
from jax.sharding import PartitionSpec as P


F32, BF16, I32 = jnp.float32, jnp.bfloat16, jnp.int32
ROWS = 16
FORWARD_STEP = 32
INVERSE_STEP = 16


def turn(a, b):
    return a[0] * b[0] - a[1] * b[1], a[1] * b[0] + a[0] * b[1]


def angles(multiples, waves, samples):
    phase = ((multiples * waves) & (samples - 1)).astype(F32) * (2.0 * math.pi / samples)
    return jnp.cos(phase), jnp.sin(phase)


def row_of(pair, k):
    return pair[0][k : k + 1], pair[1][k : k + 1]


def build_forward(even, odd, fine):
    count = even.shape[1]
    part = count // 2
    samples = 8 * count
    scale = 1.0 / math.sqrt(samples)
    first, ahead = [], []
    for k, rest in enumerate((0, 2, 1, 5)):
        row = lax.broadcasted_iota(I32, (8, count), 0)
        lane = lax.broadcasted_iota(I32, (8, count), 1)
        wave = 8 * lane + rest
        if k == 0:
            wave = jnp.where(lane < part, 8 * lane, 8 * (lane - part) + 4)
        columns = slice(k * count, (k + 1) * count)
        base = angles(row, wave, samples)
        jumps = angles(jnp.left_shift(8, jnp.minimum(row, 2)), wave, samples)
        base = (base[0] * scale, base[1] * scale)
        fine[0, 0:8, columns], fine[1, 0:8, columns] = base
        more = turn(base, row_of(jumps, 0))
        fine[0, 8:16, columns], fine[1, 8:16, columns] = more
        jump = row_of(jumps, 1)
        fine[0, 16:24, columns], fine[1, 16:24, columns] = turn(base, jump)
        fine[0, 24:32, columns], fine[1, 24:32, columns] = turn(more, jump)
        ahead.append(row_of(jumps, 2))
        first.append((jnp.ones((1, count), F32), jnp.zeros((1, count), F32)))

    def step(i, coarse):
        rows = pl.ds(i * FORWARD_STEP, FORWARD_STEP)
        for k in range(4):
            columns = slice(k * count, (k + 1) * count)
            cosine, sine = turn((fine[0, :, columns], fine[1, :, columns]), coarse[k])
            if k == 0:
                for g in range(2):
                    even[g, rows, :part] = cosine[:, g * part : (g + 1) * part].astype(BF16)
                    even[g, rows, part:] = (-sine[:, g * part : (g + 1) * part]).astype(BF16)
            else:
                odd[k - 1, rows, :count] = cosine.astype(BF16)
                odd[k - 1, rows, count:] = sine.astype(BF16)
        return [turn(a, b) for a, b in zip(coarse, ahead)]

    lax.fori_loop(0, count // FORWARD_STEP, step, first)


def forward_kernel(rx, xl, even, odd, fine):
    build_forward(even, odd, fine)


def inverse_kernel(even, odd, fine):
    count = even.shape[1]
    part = count // 2
    samples = 8 * count
    scale = 1.0 / math.sqrt(samples // 2)
    row = lax.broadcasted_iota(I32, (8, count), 0)
    time = lax.broadcasted_iota(I32, (8, count), 1)
    base = angles(8 * row, time, samples)
    jumps = angles(jnp.where(row == 0, 64, jnp.where(row == 1, 128, row - 1)), time, samples)
    base = (base[0] * scale, base[1] * scale)
    base = (base, turn(base, row_of(jumps, 0)))
    for k, rest in enumerate((0, 4, 2, 1, 5)):
        for half in range(2):
            value = turn(base[half], row_of(jumps, 1 + rest)) if rest else base[half]
            rows = slice(8 * half, 8 * half + 8)
            fine[0, k, rows, :], fine[1, k, rows, :] = value
    ahead = row_of(jumps, 1)
    sign = 1.0 - 2.0 * (time[:1] & 1).astype(F32)

    def step(i, coarse):
        rows = pl.ds(i * INVERSE_STEP, INVERSE_STEP)
        later = pl.ds(part + i * INVERSE_STEP, INVERSE_STEP)
        for k in range(5):
            cosine, sine = turn((fine[0, k], fine[1, k]), coarse)
            if k < 2:
                even[k, rows, :] = cosine.astype(BF16)
                even[k, later, :] = (-sine).astype(BF16)
            else:
                odd[k - 2, rows, :count] = cosine.astype(BF16)
                odd[k - 2, rows, count:] = sine.astype(BF16)
                odd[k - 2, later, :count] = (cosine * sign).astype(BF16)
                odd[k - 2, later, count:] = (sine * sign).astype(BF16)
        return turn(coarse, ahead)

    first = (jnp.ones((1, count), F32), jnp.zeros((1, count), F32))
    lax.fori_loop(0, part // INVERSE_STEP, step, first)


def filters_kernel(filters, out):
    count = filters.shape[1]
    part = count // 8
    column = lax.broadcasted_iota(I32, (count, count), 1)
    block, inner = column // part, column % part
    rest = jnp.zeros_like(column)
    for k, value in enumerate((0, 4, 2, 6, 1, 7, 5, 3)):
        rest = jnp.where(block == k, value, rest)
    upper = ((block == 3) | (block == 5) | (block == 7)).astype(I32)
    source = 8 * jnp.where(upper == 1, part - 1 - inner, inner) + rest
    move = (lax.broadcasted_iota(I32, (count, count), 0) == source).astype(F32).astype(BF16)
    left = filters[...]
    moved = jnp.zeros((2, count), F32)
    for _ in range(3):
        piece = left.astype(BF16)
        left = left - piece.astype(F32)
        moved = moved + jnp.dot(piece, move, preferred_element_type=F32)
    out[0:1, :] = moved[0:1]
    out[1:2, :] = jnp.where(upper[:1] == 1, -moved[1:2], moved[1:2])


def split(x):
    quarter = x.shape[-1] // 4
    half = quarter // 2
    x0, x1, x2, x3 = (x[:, q * quarter : (q + 1) * quarter].astype(F32) for q in range(4))
    first, second = x0 + x2, x1 + x3
    p, q = first + second, first - second
    re, im = x0 - x2, x3 - x1
    root = math.sqrt(0.5)
    turned_re = root * (re[:, half:] + im[:, half:])
    turned_im = root * (im[:, half:] - re[:, half:])
    re, im = re[:, :half], im[:, :half]
    return (
        (p[:, :half] + p[:, half:]).astype(BF16),
        (p[:, :half] - p[:, half:]).astype(BF16),
        (q[:, :half].astype(BF16), (-q[:, half:]).astype(BF16)),
        ((re + turned_re).astype(BF16), (im + turned_im).astype(BF16)),
        ((re - turned_re).astype(BF16), (im - turned_im).astype(BF16)),
    )


def transform(parts, even, odd):
    rows = parts[0].shape[0]
    count = even.shape[1]
    dot = functools.partial(jnp.dot, preferred_element_type=F32)
    for g in range(2):
        yield dot(parts[g], even[g])
    for g in range(3):
        both = dot(jnp.concatenate(parts[2 + g], axis=0), odd[g])
        yield both[:rows, :count] + both[rows:, count:]
        yield both[rows:, :count] - both[:rows, count:]


def groups(samples):
    count = samples // 8
    part = count // 2
    full = [(2 * count + 2 * g * count, count, count) for g in range(3)]
    return [(0, part, part), (count, part, part), *full]


def ring_place(chip):
    return jnp.where(chip % 2 == 0, chip // 2, 7 - chip // 2)


def setup_kernel(per_device, aper, ringed, rx, place, own, other, notes, notes_other, even, odd, out, token, data, arriving):
    rec_dev, samples = own.shape
    copies = [
        pltpu.make_async_copy(source, data.at[k * rec_dev : (k + 1) * rec_dev], arriving.at[k])
        for k, source in enumerate((own, other))
    ]
    for copy in copies:
        copy.start()
    core = place[0]
    slots = 2 * rec_dev
    outs = slots // aper
    out_dev = outs // 2
    earlier = (
        lax.broadcasted_iota(I32, (rec_dev, rec_dev), 0)
        < lax.broadcasted_iota(I32, (rec_dev, rec_dev), 1)
    ).astype(F32).astype(BF16)
    lines = rec_dev // aper
    sides = [
        jnp.concatenate([note[k : k + 1, :] for k in range(lines)], axis=1)
        for note in (notes, notes_other)
    ]
    ranks, totals = [], []
    for owner in sides:
        mine = (owner == core).astype(F32)
        rank = jnp.dot(
            jnp.broadcast_to(mine, (8, rec_dev)).astype(BF16), earlier, preferred_element_type=F32
        )
        ranks.append(rank[:1])
        totals.append(jnp.sum(mine, axis=1, keepdims=True))
    position = lax.broadcasted_iota(I32, (1, rec_dev), 1)
    slot_row = lax.broadcasted_iota(I32, (slots, rec_dev), 0)
    picks = []
    for side in range(2):
        second = core != side
        before = (ranks[side] + jnp.where(second, totals[1 - side], 0.0)).astype(I32)
        index = position + jnp.where(second, rec_dev, 0)
        slot = jnp.where(sides[side] == core, before, rec_dev + index - before)
        picks.append((slot_row == slot).astype(F32).astype(BF16))
    picks = jnp.concatenate(picks, axis=1)
    index = lax.broadcasted_iota(I32, (aper, aper), 0)
    if ringed:
        chunk, inner = index // ROWS, index % ROWS
        offset = (chunk + 1) // 2
        half = jnp.where((chunk % 2 == 0) & (chunk > 0), 1 - core, core)
        spot = ring_place(rx[0]) + jnp.where(core == 0, 8 - offset, offset)
        spot = spot % 8
        chip = jnp.where(spot < 4, 2 * spot, 15 - 2 * spot)
        trace = (2 * chip + half) * ROWS + inner
    else:
        trace = (index // per_device * 2 + core) * per_device + index % per_device
    rows = []
    for r in range(outs):
        line = lines + r % out_dev
        entry = (notes if r < out_dev else notes_other)[line : line + 1, :]
        match = (trace == entry).astype(F32).astype(BF16)
        pick = picks[r * aper : (r + 1) * aper]
        rows.append(jnp.dot(match, pick, preferred_element_type=F32).astype(BF16))
    placed = jnp.concatenate(rows, axis=0)
    for copy in copies:
        copy.wait()
    routed = jnp.dot(placed, data[...], preferred_element_type=F32)
    first = 0
    for block in transform(split(routed), even, odd):
        width = block.shape[1]
        block = block.astype(BF16).reshape(outs, aper // ROWS, ROWS, width)
        for r in range(outs):
            out[:, r, :, first : first + width] = block[r]
        first += width
    token[...] = jnp.zeros(token.shape, F32)


def sum_rows(values):
    row = lax.broadcasted_iota(I32, values[0].shape, 0)
    for shift in (4, 2, 1):
        upper = row % (2 * shift) < shift
        half = len(values) // 2
        joined = []
        for a, b in zip(values[:half], values[half:]):
            if shift == 4:
                rolled = pltpu.roll(jnp.where(upper, b, a), 4, 0)
            else:
                rolled = jnp.where(upper, pltpu.roll(a, 8 - shift, 0), pltpu.roll(b, shift, 0))
            joined.append(jnp.where(upper, a, b) + rolled)
        values = joined
    return values[0]


def products_kernel(chunks, count, with_total, extra, *refs):
    pieces = refs[:count]
    even, odd, spectra = refs[count : count + 3]
    totals = refs[count + 3 : count + 3 + 2 * with_total]
    outs = refs[count + 3 + 2 * with_total + extra : -1]
    work = refs[-1]
    samples = work.shape[1]
    number = spectra.shape[1]
    rows = work.shape[0] // len(chunks)
    sources = rows // ROWS
    data = jnp.concatenate([x[...].reshape(-1, samples) for x in pieces], axis=0)
    first = 0
    for block in transform(split(data), even, odd):
        work[:, first : first + block.shape[1]] = block
        first += block.shape[1]
    if len(outs) > 2:
        outs[2][...] = jnp.zeros(outs[2].shape, F32)
    for start, distance, width in groups(samples):
        for block in range(width // 128):
            re = pl.ds(start + block * 128, 128)
            im = pl.ds(start + distance + block * 128, 128)
            sums = {}
            for c in range(len(chunks)):
                for r in range(number):
                    right = [spectra[chunks[c], r, :, k].astype(F32) for k in (re, im)]
                    for h in range(ROWS // 8):
                        b_re, b_im = (b[8 * h : 8 * h + 8] for b in right)
                        for s in range(sources):
                            top = c * rows + s * ROWS + h * 8
                            a_re, a_im = work[top : top + 8, re], work[top : top + 8, im]
                            x = a_re * b_re - a_im * b_im
                            y = a_re * b_im + a_im * b_re
                            if (s, r) in sums:
                                x, y = x + sums[s, r][0], y + sums[s, r][1]
                            sums[s, r] = (x, y)
            share = number // 2
            for i in range(2):
                keys = [(s, i * share + r) for r in range(share) for s in range(sources)]
                for part, columns in enumerate((re, im)):
                    value = sum_rows([sums[key][part] for key in keys])
                    if with_total:
                        value = value + totals[i][:, columns]
                    outs[i][:, columns] = value


def finish_kernel(scale, filters, mine, arrived, even, odd, out):
    count = even.shape[1]
    sources, out_dev, samples = out.shape
    raw = mine[...] + arrived[...]
    rows = raw.shape[0]
    dot = functools.partial(jnp.dot, preferred_element_type=F32)
    waves, column = [], 0
    for g, (start, distance, width) in enumerate(groups(samples)):
        g_re = filters[0:1, column : column + width] * scale
        g_im = filters[1:2, column : column + width] * scale
        column += width
        x = raw[:, start : start + width]
        y = raw[:, start + distance : start + distance + width]
        x, y = g_re * x - g_im * y, g_re * y + g_im * x
        if g < 2:
            waves.append(dot(jnp.concatenate([x, y], axis=1).astype(BF16), even[g]))
        else:
            both = dot(jnp.concatenate([x, y], axis=0).astype(BF16), odd[g - 2])
            waves.append(both[:rows, :count] - both[rows:, count:])
            waves.append(both[:rows, count:] + both[rows:, :count])
    a, b, h_re, h_im, v_re, v_im, w_re, w_im = waves
    root = math.sqrt(0.5)
    plus, minus = a + b, a - b
    u_re, u_im = v_re + w_re, v_im + w_im
    v_re, v_im = v_re - w_re, v_im - w_im
    less, more = root * (v_re - v_im), root * (v_re + v_im)
    results = (
        plus + h_re + u_re,
        minus - h_im + less,
        plus - h_re - u_im,
        minus + h_im - more,
        plus + h_re - u_re,
        minus - h_im - less,
        plus - h_re + u_im,
        minus + h_im + more,
    )
    for k, value in enumerate(results):
        value = value.reshape(out_dev, sources, count)
        for r in range(out_dev):
            out[:, r, k * count : (k + 1) * count] = value[r].astype(BF16)


def call(kernel, out_shape, kinds, scratch=(), limit=24, cost=1):
    spaces = {"s": pltpu.SMEM, "v": pltpu.VMEM, "a": pl.ANY}
    specs = [pl.BlockSpec(memory_space=spaces[k]) for k in kinds]
    return pl.pallas_call(
        kernel,
        out_shape=out_shape,
        in_specs=specs,
        out_specs=[pl.BlockSpec(memory_space=pltpu.VMEM)] * len(out_shape),
        cost_estimate=pl.CostEstimate(
            flops=cost * 10**9, transcendentals=0, bytes_accessed=cost * 3 * 10**6
        ),
        scratch_shapes=list(scratch),
        compiler_params=pltpu.CompilerParams(vmem_limit_bytes=limit << 20),
    )


def per_device(ring_size, source_traces, surface_filter, records, owners, aperture):
    sources, own_traces, samples = source_traces.shape
    out_dev, aper = aperture.shape
    rec_dev = records.shape[0]
    count = samples // 8
    struct = jax.ShapeDtypeStruct
    rx, xl = (lax.axis_index(axis).astype(I32).reshape(1) for axis in ("rx", "xl"))
    outs = 2 * out_dev
    chunks = aper // ROWS
    token = struct((8, 128), F32)

    def after(token, *values):
        return lax.optimization_barrier((*values, token))

    def swap(x):
        return lax.ppermute(x, "xl", [(0, 1), (1, 0)])

    notes = jnp.concatenate([owners.reshape(-1, aper), aperture], axis=0)
    table_shapes = [struct((2, count, count), BF16), struct((3, count, 2 * count), BF16)]
    fine = [pltpu.VMEM((2, FORWARD_STEP, 4 * count), F32)]
    tables = call(forward_kernel, table_shapes, "ss", fine)(rx, xl)

    ringed = ring_size == 8 and own_traces == ROWS and aper == 8 * ROWS

    def setup():
        return call(
            functools.partial(setup_kernel, own_traces, aper, ringed),
            [struct((chunks, outs, ROWS, samples), BF16), token],
            "ssaavvvv",
            [pltpu.VMEM((2 * rec_dev, samples), BF16), pltpu.SemaphoreType.DMA((2,))],
            cost=4,
        )(rx, xl, records, swap(records), notes, swap(notes), *tables)

    def arrange(filters):
        return call(filters_kernel, [struct(filters.shape, F32)], "v")(filters)[0]

    def add(pieces, numbers, totals, extra=(), mark=True):
        kernel = functools.partial(
            products_kernel, numbers, len(pieces), bool(totals), len(extra)
        )
        arguments = [*pieces, *tables, spectra, *totals, *extra]
        row_shape = struct((out_dev * sources, samples), F32)
        result = call(
            kernel,
            [row_shape, row_shape, *[token] * mark],
            "v" * len(arguments),
            [pltpu.VMEM((len(numbers) * sources * ROWS, samples), F32)],
        )(*arguments)
        return result[:2], result[-1]

    if ringed:
        order = [0, 2, 4, 6, 7, 5, 3, 1]
        same, cross = [], []
        for i in range(8):
            here, above, below = order[i], order[(i + 1) % 8], order[i - 1]
            same += [(2 * here, 2 * above), (2 * here + 1, 2 * below + 1)]
            cross += [(2 * here + 1, 2 * above), (2 * here, 2 * below + 1)]

        def send(x, pairs=same):
            return lax.ppermute(x, ("rx", "xl"), pairs)

        a1, b1 = send(source_traces), send(source_traces, cross)
        spectra, done = setup()
        a_held, first = after(done, a1)
        b_held, second = after(done, b1)
        a2, b2 = send(a_held), send(b_held)
        totals, _ = add([source_traces], [0], [], [first, second], mark=False)
        totals, done = add([a1, b1], [1, 2], totals)
        filters = arrange(surface_filter)
        a_held, first = after(done, a2)
        b_held, filters, second = after(done, b2, filters)
        a3, b3 = send(a_held), send(b_held)
        totals, _ = add([a2, b2], [3, 4], totals, [first, second], mark=False)
        a4 = send(a3)
        totals, _ = add([a3, b3], [5, 6], totals, mark=False)
        (mine, theirs), _ = add([a4], [7], totals, mark=False)
    else:
        spectra, _ = setup()
        gathered = lax.all_gather(source_traces, "rx", axis=1, tiled=True)
        parts = [gathered[:, k * ROWS : (k + 1) * ROWS] for k in range(chunks)]
        totals = []
        for k in range(0, chunks, 2):
            totals, _ = add(parts[k : k + 2], [k, k + 1], totals, mark=False)
        mine, theirs = totals
        filters = arrange(surface_filter)

    fine = [pltpu.VMEM((2, 5, INVERSE_STEP, count), F32)]
    inverse = call(inverse_kernel, table_shapes, "", fine)()
    return call(
        functools.partial(finish_kernel, 1.0 / math.sqrt(aper)),
        [struct((sources, out_dev, samples), BF16)],
        "vvvvv",
    )(filters, mine, swap(theirs), *inverse)[0]


def solution(mesh):
    in_specs = (
        P(None, ("groups", "rx", "xl"), None),
        P(),
        P(("groups", "rx", "xl"), None),
        P(("groups", "rx", "xl")),
        P(("groups", "rx", "xl"), None),
    )
    out_specs = P(None, ("groups", "rx", "xl"), None)
    return jax.shard_map(
        functools.partial(per_device, mesh.shape["rx"]),
        mesh=mesh,
        in_specs=in_specs,
        out_specs=out_specs,
        check_vma=False,
    )
```

```python
import functools
import math

import jax
import jax.numpy as jnp
from jax import lax
from jax.experimental import pallas as pl
from jax.experimental.pallas import tpu as pltpu
from jax.sharding import PartitionSpec as P


F32, BF16, I32 = jnp.float32, jnp.bfloat16, jnp.int32
ROWS = 16
FORWARD_STEP = 32
INVERSE_STEP = 16


def turn(a, b):
    return a[0] * b[0] - a[1] * b[1], a[1] * b[0] + a[0] * b[1]


def angles(multiples, waves, samples):
    phase = ((multiples * waves) & (samples - 1)).astype(F32) * (2.0 * math.pi / samples)
    return jnp.cos(phase), jnp.sin(phase)


def row_of(pair, k):
    return pair[0][k : k + 1], pair[1][k : k + 1]


def build_forward(even, odd, fine):
    count = even.shape[1]
    part = count // 2
    samples = 8 * count
    scale = 1.0 / math.sqrt(samples)
    first, ahead = [], []
    for k, rest in enumerate((0, 2, 1, 5)):
        row = lax.broadcasted_iota(I32, (8, count), 0)
        lane = lax.broadcasted_iota(I32, (8, count), 1)
        wave = 8 * lane + rest
        if k == 0:
            wave = jnp.where(lane < part, 8 * lane, 8 * (lane - part) + 4)
        columns = slice(k * count, (k + 1) * count)
        base = angles(row, wave, samples)
        jumps = angles(jnp.left_shift(8, jnp.minimum(row, 2)), wave, samples)
        base = (base[0] * scale, base[1] * scale)
        fine[0, 0:8, columns], fine[1, 0:8, columns] = base
        more = turn(base, row_of(jumps, 0))
        fine[0, 8:16, columns], fine[1, 8:16, columns] = more
        jump = row_of(jumps, 1)
        fine[0, 16:24, columns], fine[1, 16:24, columns] = turn(base, jump)
        fine[0, 24:32, columns], fine[1, 24:32, columns] = turn(more, jump)
        ahead.append(row_of(jumps, 2))
        first.append((jnp.ones((1, count), F32), jnp.zeros((1, count), F32)))

    def step(i, coarse):
        rows = pl.ds(i * FORWARD_STEP, FORWARD_STEP)
        for k in range(4):
            columns = slice(k * count, (k + 1) * count)
            cosine, sine = turn((fine[0, :, columns], fine[1, :, columns]), coarse[k])
            if k == 0:
                for g in range(2):
                    even[g, rows, :part] = cosine[:, g * part : (g + 1) * part].astype(BF16)
                    even[g, rows, part:] = (-sine[:, g * part : (g + 1) * part]).astype(BF16)
            else:
                odd[k - 1, rows, :count] = cosine.astype(BF16)
                odd[k - 1, rows, count:] = sine.astype(BF16)
        return [turn(a, b) for a, b in zip(coarse, ahead)]

    lax.fori_loop(0, count // FORWARD_STEP, step, first)


def forward_kernel(rx, xl, even, odd, fine):
    build_forward(even, odd, fine)


def inverse_kernel(even, odd, fine):
    count = even.shape[1]
    part = count // 2
    samples = 8 * count
    scale = 1.0 / math.sqrt(samples // 2)
    row = lax.broadcasted_iota(I32, (8, count), 0)
    time = lax.broadcasted_iota(I32, (8, count), 1)
    base = angles(8 * row, time, samples)
    jumps = angles(jnp.where(row == 0, 64, jnp.where(row == 1, 128, row - 1)), time, samples)
    base = (base[0] * scale, base[1] * scale)
    base = (base, turn(base, row_of(jumps, 0)))
    for k, rest in enumerate((0, 4, 2, 1, 5)):
        for half in range(2):
            value = turn(base[half], row_of(jumps, 1 + rest)) if rest else base[half]
            rows = slice(8 * half, 8 * half + 8)
            fine[0, k, rows, :], fine[1, k, rows, :] = value
    ahead = row_of(jumps, 1)
    sign = 1.0 - 2.0 * (time[:1] & 1).astype(F32)

    def step(i, coarse):
        rows = pl.ds(i * INVERSE_STEP, INVERSE_STEP)
        later = pl.ds(part + i * INVERSE_STEP, INVERSE_STEP)
        for k in range(5):
            cosine, sine = turn((fine[0, k], fine[1, k]), coarse)
            if k < 2:
                even[k, rows, :] = cosine.astype(BF16)
                even[k, later, :] = (-sine).astype(BF16)
            else:
                odd[k - 2, rows, :count] = cosine.astype(BF16)
                odd[k - 2, rows, count:] = sine.astype(BF16)
                odd[k - 2, later, :count] = (cosine * sign).astype(BF16)
                odd[k - 2, later, count:] = (sine * sign).astype(BF16)
        return turn(coarse, ahead)

    first = (jnp.ones((1, count), F32), jnp.zeros((1, count), F32))
    lax.fori_loop(0, part // INVERSE_STEP, step, first)


def filters_kernel(filters, out):
    count = filters.shape[1]
    part = count // 8
    column = lax.broadcasted_iota(I32, (count, count), 1)
    block, inner = column // part, column % part
    rest = jnp.zeros_like(column)
    for k, value in enumerate((0, 4, 2, 6, 1, 7, 5, 3)):
        rest = jnp.where(block == k, value, rest)
    upper = ((block == 3) | (block == 5) | (block == 7)).astype(I32)
    source = 8 * jnp.where(upper == 1, part - 1 - inner, inner) + rest
    move = (lax.broadcasted_iota(I32, (count, count), 0) == source).astype(F32).astype(BF16)
    left = filters[...]
    moved = jnp.zeros((2, count), F32)
    for _ in range(3):
        piece = left.astype(BF16)
        left = left - piece.astype(F32)
        moved = moved + jnp.dot(piece, move, preferred_element_type=F32)
    out[0:1, :] = moved[0:1]
    out[1:2, :] = jnp.where(upper[:1] == 1, -moved[1:2], moved[1:2])


def split(x):
    quarter = x.shape[-1] // 4
    half = quarter // 2
    x0, x1, x2, x3 = (x[:, q * quarter : (q + 1) * quarter].astype(F32) for q in range(4))
    first, second = x0 + x2, x1 + x3
    p, q = first + second, first - second
    re, im = x0 - x2, x3 - x1
    root = math.sqrt(0.5)
    turned_re = root * (re[:, half:] + im[:, half:])
    turned_im = root * (im[:, half:] - re[:, half:])
    re, im = re[:, :half], im[:, :half]
    return (
        (p[:, :half] + p[:, half:]).astype(BF16),
        (p[:, :half] - p[:, half:]).astype(BF16),
        (q[:, :half].astype(BF16), (-q[:, half:]).astype(BF16)),
        ((re + turned_re).astype(BF16), (im + turned_im).astype(BF16)),
        ((re - turned_re).astype(BF16), (im - turned_im).astype(BF16)),
    )


def transform(parts, even, odd):
    rows = parts[0].shape[0]
    count = even.shape[1]
    dot = functools.partial(jnp.dot, preferred_element_type=F32)
    for g in range(2):
        yield dot(parts[g], even[g])
    for g in range(3):
        both = dot(jnp.concatenate(parts[2 + g], axis=0), odd[g])
        yield both[:rows, :count] + both[rows:, count:]
        yield both[rows:, :count] - both[:rows, count:]


def groups(samples):
    count = samples // 8
    part = count // 2
    full = [(2 * count + 2 * g * count, count, count) for g in range(3)]
    return [(0, part, part), (count, part, part), *full]


def ring_place(chip):
    return jnp.where(chip % 2 == 0, chip // 2, 7 - chip // 2)


def setup_kernel(per_device, aper, ringed, rx, place, own, other, notes, notes_other, even, odd, out, token):
    rec_dev, samples = own.shape
    core = place[0]
    slots = 2 * rec_dev
    outs = slots // aper
    out_dev = outs // 2
    earlier = (
        lax.broadcasted_iota(I32, (rec_dev, rec_dev), 0)
        < lax.broadcasted_iota(I32, (rec_dev, rec_dev), 1)
    ).astype(F32).astype(BF16)
    lines = rec_dev // aper
    sides = [
        jnp.concatenate([note[k : k + 1, :] for k in range(lines)], axis=1)
        for note in (notes, notes_other)
    ]
    ranks, totals = [], []
    for owner in sides:
        mine = (owner == core).astype(F32)
        rank = jnp.dot(
            jnp.broadcast_to(mine, (8, rec_dev)).astype(BF16), earlier, preferred_element_type=F32
        )
        ranks.append(rank[:1])
        totals.append(jnp.sum(mine, axis=1, keepdims=True))
    position = lax.broadcasted_iota(I32, (1, rec_dev), 1)
    slot_row = lax.broadcasted_iota(I32, (slots, rec_dev), 0)
    picks = []
    for side in range(2):
        second = core != side
        before = (ranks[side] + jnp.where(second, totals[1 - side], 0.0)).astype(I32)
        index = position + jnp.where(second, rec_dev, 0)
        slot = jnp.where(sides[side] == core, before, rec_dev + index - before)
        picks.append((slot_row == slot).astype(F32).astype(BF16))
    picks = jnp.concatenate(picks, axis=1)
    index = lax.broadcasted_iota(I32, (aper, aper), 0)
    if ringed:
        chunk, inner = index // ROWS, index % ROWS
        offset = (chunk + 1) // 2
        half = jnp.where((chunk % 2 == 0) & (chunk > 0), 1 - core, core)
        spot = ring_place(rx[0]) + jnp.where(core == 0, 8 - offset, offset)
        spot = spot % 8
        chip = jnp.where(spot < 4, 2 * spot, 15 - 2 * spot)
        trace = (2 * chip + half) * ROWS + inner
    else:
        trace = (index // per_device * 2 + core) * per_device + index % per_device
    rows = []
    for r in range(outs):
        line = lines + r % out_dev
        entry = (notes if r < out_dev else notes_other)[line : line + 1, :]
        match = (trace == entry).astype(F32).astype(BF16)
        pick = picks[r * aper : (r + 1) * aper]
        rows.append(jnp.dot(match, pick, preferred_element_type=F32).astype(BF16))
    placed = jnp.concatenate(rows, axis=0)
    routed = jnp.dot(placed[:, :rec_dev], own[...], preferred_element_type=F32) + jnp.dot(
        placed[:, rec_dev:], other[...], preferred_element_type=F32
    )
    first = 0
    for block in transform(split(routed), even, odd):
        width = block.shape[1]
        block = block.astype(BF16).reshape(outs, aper // ROWS, ROWS, width)
        for r in range(outs):
            out[:, r, :, first : first + width] = block[r]
        first += width
    token[...] = jnp.zeros(token.shape, F32)


def sum_rows(values):
    row = lax.broadcasted_iota(I32, values[0].shape, 0)
    for shift in (4, 2, 1):
        upper = row % (2 * shift) < shift
        half = len(values) // 2
        joined = []
        for a, b in zip(values[:half], values[half:]):
            if shift == 4:
                rolled = pltpu.roll(jnp.where(upper, b, a), 4, 0)
            else:
                rolled = jnp.where(upper, pltpu.roll(a, 8 - shift, 0), pltpu.roll(b, shift, 0))
            joined.append(jnp.where(upper, a, b) + rolled)
        values = joined
    return values[0]


def products_kernel(chunks, count, with_total, extra, *refs):
    pieces = refs[:count]
    even, odd, spectra = refs[count : count + 3]
    totals = refs[count + 3 : count + 3 + 2 * with_total]
    outs = refs[count + 3 + 2 * with_total + extra : -1]
    work = refs[-1]
    samples = work.shape[1]
    number = spectra.shape[1]
    rows = work.shape[0] // len(chunks)
    sources = rows // ROWS
    data = jnp.concatenate([x[...].reshape(-1, samples) for x in pieces], axis=0)
    first = 0
    for block in transform(split(data), even, odd):
        work[:, first : first + block.shape[1]] = block
        first += block.shape[1]
    if len(outs) > 2:
        outs[2][...] = jnp.zeros(outs[2].shape, F32)
    for start, distance, width in groups(samples):
        for block in range(width // 128):
            re = pl.ds(start + block * 128, 128)
            im = pl.ds(start + distance + block * 128, 128)
            sums = {}
            for c in range(len(chunks)):
                for r in range(number):
                    right = [spectra[chunks[c], r, :, k].astype(F32) for k in (re, im)]
                    for h in range(ROWS // 8):
                        b_re, b_im = (b[8 * h : 8 * h + 8] for b in right)
                        for s in range(sources):
                            top = c * rows + s * ROWS + h * 8
                            a_re, a_im = work[top : top + 8, re], work[top : top + 8, im]
                            x = a_re * b_re - a_im * b_im
                            y = a_re * b_im + a_im * b_re
                            if (s, r) in sums:
                                x, y = x + sums[s, r][0], y + sums[s, r][1]
                            sums[s, r] = (x, y)
            share = number // 2
            for i in range(2):
                keys = [(s, i * share + r) for r in range(share) for s in range(sources)]
                for part, columns in enumerate((re, im)):
                    value = sum_rows([sums[key][part] for key in keys])
                    if with_total:
                        value = value + totals[i][:, columns]
                    outs[i][:, columns] = value


def finish_kernel(scale, filters, mine, arrived, even, odd, out):
    count = even.shape[1]
    sources, out_dev, samples = out.shape
    raw = mine[...] + arrived[...]
    rows = raw.shape[0]
    dot = functools.partial(jnp.dot, preferred_element_type=F32)
    waves, column = [], 0
    for g, (start, distance, width) in enumerate(groups(samples)):
        g_re = filters[0:1, column : column + width] * scale
        g_im = filters[1:2, column : column + width] * scale
        column += width
        x = raw[:, start : start + width]
        y = raw[:, start + distance : start + distance + width]
        x, y = g_re * x - g_im * y, g_re * y + g_im * x
        if g < 2:
            waves.append(dot(jnp.concatenate([x, y], axis=1).astype(BF16), even[g]))
        else:
            both = dot(jnp.concatenate([x, y], axis=0).astype(BF16), odd[g - 2])
            waves.append(both[:rows, :count] - both[rows:, count:])
            waves.append(both[:rows, count:] + both[rows:, :count])
    a, b, h_re, h_im, v_re, v_im, w_re, w_im = waves
    root = math.sqrt(0.5)
    plus, minus = a + b, a - b
    u_re, u_im = v_re + w_re, v_im + w_im
    v_re, v_im = v_re - w_re, v_im - w_im
    less, more = root * (v_re - v_im), root * (v_re + v_im)
    results = (
        plus + h_re + u_re,
        minus - h_im + less,
        plus - h_re - u_im,
        minus + h_im - more,
        plus + h_re - u_re,
        minus - h_im - less,
        plus - h_re + u_im,
        minus + h_im + more,
    )
    for k, value in enumerate(results):
        value = value.reshape(out_dev, sources, count)
        for r in range(out_dev):
            out[:, r, k * count : (k + 1) * count] = value[r].astype(BF16)


def call(kernel, out_shape, kinds, scratch=(), limit=24, cost=1):
    spaces = {"s": pltpu.SMEM, "v": pltpu.VMEM, "a": pl.ANY}
    specs = [pl.BlockSpec(memory_space=spaces[k]) for k in kinds]
    return pl.pallas_call(
        kernel,
        out_shape=out_shape,
        in_specs=specs,
        out_specs=[pl.BlockSpec(memory_space=pltpu.VMEM)] * len(out_shape),
        cost_estimate=pl.CostEstimate(
            flops=cost * 10**9, transcendentals=0, bytes_accessed=cost * 3 * 10**6
        ),
        scratch_shapes=list(scratch),
        compiler_params=pltpu.CompilerParams(vmem_limit_bytes=limit << 20),
    )


def per_device(ring_size, source_traces, surface_filter, records, owners, aperture):
    sources, own_traces, samples = source_traces.shape
    out_dev, aper = aperture.shape
    rec_dev = records.shape[0]
    count = samples // 8
    struct = jax.ShapeDtypeStruct
    rx, xl = (lax.axis_index(axis).astype(I32).reshape(1) for axis in ("rx", "xl"))
    outs = 2 * out_dev
    chunks = aper // ROWS
    token = struct((8, 128), F32)

    def after(token, *values):
        return lax.optimization_barrier((*values, token))

    def swap(x):
        return lax.ppermute(x, "xl", [(0, 1), (1, 0)])

    notes = jnp.concatenate([owners.reshape(-1, aper), aperture], axis=0)
    table_shapes = [struct((2, count, count), BF16), struct((3, count, 2 * count), BF16)]
    fine = [pltpu.VMEM((2, FORWARD_STEP, 4 * count), F32)]
    tables = call(forward_kernel, table_shapes, "ss", fine)(rx, xl)

    ringed = ring_size == 8 and own_traces == ROWS and aper == 8 * ROWS

    def setup():
        return call(
            functools.partial(setup_kernel, own_traces, aper, ringed),
            [struct((chunks, outs, ROWS, samples), BF16), token],
            "ssvvvvvv",
            cost=4,
        )(rx, xl, records, swap(records), notes, swap(notes), *tables)

    def arrange(filters):
        return call(filters_kernel, [struct(filters.shape, F32)], "v")(filters)[0]

    def add(pieces, numbers, totals, extra=(), mark=True):
        kernel = functools.partial(
            products_kernel, numbers, len(pieces), bool(totals), len(extra)
        )
        arguments = [*pieces, *tables, spectra, *totals, *extra]
        row_shape = struct((out_dev * sources, samples), F32)
        result = call(
            kernel,
            [row_shape, row_shape, *[token] * mark],
            "v" * len(arguments),
            [pltpu.VMEM((len(numbers) * sources * ROWS, samples), F32)],
        )(*arguments)
        return result[:2], result[-1]

    if ringed:
        order = [0, 2, 4, 6, 7, 5, 3, 1]
        same, cross = [], []
        for i in range(8):
            here, above, below = order[i], order[(i + 1) % 8], order[i - 1]
            same += [(2 * here, 2 * above), (2 * here + 1, 2 * below + 1)]
            cross += [(2 * here + 1, 2 * above), (2 * here, 2 * below + 1)]

        def send(x, pairs=same):
            return lax.ppermute(x, ("rx", "xl"), pairs)

        a1, b1 = send(source_traces), send(source_traces, cross)
        spectra, done = setup()
        a_held, first = after(done, a1)
        a2 = send(a_held)
        totals, done = add([source_traces], [0], [], [first])
        b_held, second = after(done, b1)
        b2 = send(b_held)
        totals, done = add([a1, b1], [1, 2], totals, [second])
        filters = arrange(surface_filter)
        a_held, first = after(done, a2)
        b_held, filters, second = after(done, b2, filters)
        a3, b3 = send(a_held), send(b_held)
        totals, _ = add([a2, b2], [3, 4], totals, [first, second], mark=False)
        a4 = send(a3)
        totals, _ = add([a3, b3], [5, 6], totals, mark=False)
        (mine, theirs), _ = add([a4], [7], totals, mark=False)
    else:
        spectra, _ = setup()
        gathered = lax.all_gather(source_traces, "rx", axis=1, tiled=True)
        parts = [gathered[:, k * ROWS : (k + 1) * ROWS] for k in range(chunks)]
        totals = []
        for k in range(0, chunks, 2):
            totals, _ = add(parts[k : k + 2], [k, k + 1], totals, mark=False)
        mine, theirs = totals
        filters = arrange(surface_filter)

    fine = [pltpu.VMEM((2, 5, INVERSE_STEP, count), F32)]
    inverse = call(inverse_kernel, table_shapes, "", fine)()
    return call(
        functools.partial(finish_kernel, 1.0 / math.sqrt(aper)),
        [struct((sources, out_dev, samples), BF16)],
        "vvvvv",
    )(filters, mine, swap(theirs), *inverse)[0]


def solution(mesh):
    in_specs = (
        P(None, ("groups", "rx", "xl"), None),
        P(),
        P(("groups", "rx", "xl"), None),
        P(("groups", "rx", "xl")),
        P(("groups", "rx", "xl"), None),
    )
    out_specs = P(None, ("groups", "rx", "xl"), None)
    return jax.shard_map(
        functools.partial(per_device, mesh.shape["rx"]),
        mesh=mesh,
        in_specs=in_specs,
        out_specs=out_specs,
        check_vma=False,
    )
```

```python
import functools
import math

import jax
import jax.numpy as jnp
from jax import lax
from jax.experimental import pallas as pl
from jax.experimental.pallas import tpu as pltpu
from jax.sharding import PartitionSpec as P


F32, BF16, I32 = jnp.float32, jnp.bfloat16, jnp.int32
ROWS = 16
FORWARD_STEP = 32
INVERSE_STEP = 16


def turn(a, b):
    return a[0] * b[0] - a[1] * b[1], a[1] * b[0] + a[0] * b[1]


def angles(multiples, waves, samples):
    phase = ((multiples * waves) & (samples - 1)).astype(F32) * (2.0 * math.pi / samples)
    return jnp.cos(phase), jnp.sin(phase)


def row_of(pair, k):
    return pair[0][k : k + 1], pair[1][k : k + 1]


def build_forward(even, odd, fine):
    count = even.shape[1]
    part = count // 2
    samples = 8 * count
    scale = 1.0 / math.sqrt(samples)
    first, ahead = [], []
    for k, rest in enumerate((0, 2, 1, 5)):
        row = lax.broadcasted_iota(I32, (8, count), 0)
        lane = lax.broadcasted_iota(I32, (8, count), 1)
        wave = 8 * lane + rest
        if k == 0:
            wave = jnp.where(lane < part, 8 * lane, 8 * (lane - part) + 4)
        columns = slice(k * count, (k + 1) * count)
        base = angles(row, wave, samples)
        jumps = angles(jnp.left_shift(8, jnp.minimum(row, 2)), wave, samples)
        base = (base[0] * scale, base[1] * scale)
        fine[0, 0:8, columns], fine[1, 0:8, columns] = base
        more = turn(base, row_of(jumps, 0))
        fine[0, 8:16, columns], fine[1, 8:16, columns] = more
        jump = row_of(jumps, 1)
        fine[0, 16:24, columns], fine[1, 16:24, columns] = turn(base, jump)
        fine[0, 24:32, columns], fine[1, 24:32, columns] = turn(more, jump)
        ahead.append(row_of(jumps, 2))
        first.append((jnp.ones((1, count), F32), jnp.zeros((1, count), F32)))

    def step(i, coarse):
        rows = pl.ds(i * FORWARD_STEP, FORWARD_STEP)
        for k in range(4):
            columns = slice(k * count, (k + 1) * count)
            cosine, sine = turn((fine[0, :, columns], fine[1, :, columns]), coarse[k])
            if k == 0:
                for g in range(2):
                    even[g, rows, :part] = cosine[:, g * part : (g + 1) * part].astype(BF16)
                    even[g, rows, part:] = (-sine[:, g * part : (g + 1) * part]).astype(BF16)
            else:
                odd[k - 1, rows, :count] = cosine.astype(BF16)
                odd[k - 1, rows, count:] = sine.astype(BF16)
        return [turn(a, b) for a, b in zip(coarse, ahead)]

    lax.fori_loop(0, count // FORWARD_STEP, step, first)


def forward_kernel(rx, xl, even, odd, fine):
    build_forward(even, odd, fine)


def inverse_kernel(even, odd, fine):
    count = even.shape[1]
    part = count // 2
    samples = 8 * count
    scale = 1.0 / math.sqrt(samples // 2)
    row = lax.broadcasted_iota(I32, (8, count), 0)
    time = lax.broadcasted_iota(I32, (8, count), 1)
    base = angles(8 * row, time, samples)
    jumps = angles(jnp.where(row == 0, 64, jnp.where(row == 1, 128, row - 1)), time, samples)
    base = (base[0] * scale, base[1] * scale)
    base = (base, turn(base, row_of(jumps, 0)))
    for k, rest in enumerate((0, 4, 2, 1, 5)):
        for half in range(2):
            value = turn(base[half], row_of(jumps, 1 + rest)) if rest else base[half]
            rows = slice(8 * half, 8 * half + 8)
            fine[0, k, rows, :], fine[1, k, rows, :] = value
    ahead = row_of(jumps, 1)
    sign = 1.0 - 2.0 * (time[:1] & 1).astype(F32)

    def step(i, coarse):
        rows = pl.ds(i * INVERSE_STEP, INVERSE_STEP)
        later = pl.ds(part + i * INVERSE_STEP, INVERSE_STEP)
        for k in range(5):
            cosine, sine = turn((fine[0, k], fine[1, k]), coarse)
            if k < 2:
                even[k, rows, :] = cosine.astype(BF16)
                even[k, later, :] = (-sine).astype(BF16)
            else:
                odd[k - 2, rows, :count] = cosine.astype(BF16)
                odd[k - 2, rows, count:] = sine.astype(BF16)
                odd[k - 2, later, :count] = (cosine * sign).astype(BF16)
                odd[k - 2, later, count:] = (sine * sign).astype(BF16)
        return turn(coarse, ahead)

    first = (jnp.ones((1, count), F32), jnp.zeros((1, count), F32))
    lax.fori_loop(0, part // INVERSE_STEP, step, first)


def filters_kernel(filters, out):
    count = filters.shape[1]
    part = count // 8
    column = lax.broadcasted_iota(I32, (count, count), 1)
    block, inner = column // part, column % part
    rest = jnp.zeros_like(column)
    for k, value in enumerate((0, 4, 2, 6, 1, 7, 5, 3)):
        rest = jnp.where(block == k, value, rest)
    upper = ((block == 3) | (block == 5) | (block == 7)).astype(I32)
    source = 8 * jnp.where(upper == 1, part - 1 - inner, inner) + rest
    move = (lax.broadcasted_iota(I32, (count, count), 0) == source).astype(F32).astype(BF16)
    left = filters[...]
    moved = jnp.zeros((2, count), F32)
    for _ in range(3):
        piece = left.astype(BF16)
        left = left - piece.astype(F32)
        moved = moved + jnp.dot(piece, move, preferred_element_type=F32)
    out[0:1, :] = moved[0:1]
    out[1:2, :] = jnp.where(upper[:1] == 1, -moved[1:2], moved[1:2])


def split(x):
    quarter = x.shape[-1] // 4
    half = quarter // 2
    x0, x1, x2, x3 = (x[:, q * quarter : (q + 1) * quarter].astype(F32) for q in range(4))
    first, second = x0 + x2, x1 + x3
    p, q = first + second, first - second
    re, im = x0 - x2, x3 - x1
    root = math.sqrt(0.5)
    turned_re = root * (re[:, half:] + im[:, half:])
    turned_im = root * (im[:, half:] - re[:, half:])
    re, im = re[:, :half], im[:, :half]
    return (
        (p[:, :half] + p[:, half:]).astype(BF16),
        (p[:, :half] - p[:, half:]).astype(BF16),
        (q[:, :half].astype(BF16), (-q[:, half:]).astype(BF16)),
        ((re + turned_re).astype(BF16), (im + turned_im).astype(BF16)),
        ((re - turned_re).astype(BF16), (im - turned_im).astype(BF16)),
    )


def transform(parts, even, odd):
    rows = parts[0].shape[0]
    count = even.shape[1]
    dot = functools.partial(jnp.dot, preferred_element_type=F32)
    for g in range(2):
        yield dot(parts[g], even[g])
    for g in range(3):
        both = dot(jnp.concatenate(parts[2 + g], axis=0), odd[g])
        yield both[:rows, :count] + both[rows:, count:]
        yield both[rows:, :count] - both[:rows, count:]


def groups(samples):
    count = samples // 8
    part = count // 2
    full = [(2 * count + 2 * g * count, count, count) for g in range(3)]
    return [(0, part, part), (count, part, part), *full]


def ring_place(chip):
    return jnp.where(chip % 2 == 0, chip // 2, 7 - chip // 2)


def setup_kernel(per_device, aper, ringed, rx, place, own, other, notes, notes_other, even, odd, out, token):
    rec_dev, samples = own.shape
    core = place[0]
    slots = 2 * rec_dev
    outs = slots // aper
    out_dev = outs // 2
    earlier = (
        lax.broadcasted_iota(I32, (rec_dev, rec_dev), 0)
        < lax.broadcasted_iota(I32, (rec_dev, rec_dev), 1)
    ).astype(F32).astype(BF16)
    lines = rec_dev // aper
    sides = [
        jnp.concatenate([note[k : k + 1, :] for k in range(lines)], axis=1)
        for note in (notes, notes_other)
    ]
    ranks, totals = [], []
    for owner in sides:
        mine = (owner == core).astype(F32)
        rank = jnp.dot(
            jnp.broadcast_to(mine, (8, rec_dev)).astype(BF16), earlier, preferred_element_type=F32
        )
        ranks.append(rank[:1])
        totals.append(jnp.sum(mine, axis=1, keepdims=True))
    position = lax.broadcasted_iota(I32, (1, rec_dev), 1)
    slot_row = lax.broadcasted_iota(I32, (slots, rec_dev), 0)
    picks = []
    for side in range(2):
        second = core != side
        before = (ranks[side] + jnp.where(second, totals[1 - side], 0.0)).astype(I32)
        index = position + jnp.where(second, rec_dev, 0)
        slot = jnp.where(sides[side] == core, before, rec_dev + index - before)
        picks.append((slot_row == slot).astype(F32).astype(BF16))
    picks = jnp.concatenate(picks, axis=1)
    index = lax.broadcasted_iota(I32, (aper, aper), 0)
    if ringed:
        chunk, inner = index // ROWS, index % ROWS
        offset = (chunk + 1) // 2
        half = jnp.where((chunk % 2 == 0) & (chunk > 0), 1 - core, core)
        spot = ring_place(rx[0]) + jnp.where(core == 0, 8 - offset, offset)
        spot = spot % 8
        chip = jnp.where(spot < 4, 2 * spot, 15 - 2 * spot)
        trace = (2 * chip + half) * ROWS + inner
    else:
        trace = (index // per_device * 2 + core) * per_device + index % per_device
    rows = []
    for r in range(outs):
        line = lines + r % out_dev
        entry = (notes if r < out_dev else notes_other)[line : line + 1, :]
        match = (trace == entry).astype(F32).astype(BF16)
        pick = picks[r * aper : (r + 1) * aper]
        rows.append(jnp.dot(match, pick, preferred_element_type=F32).astype(BF16))
    placed = jnp.concatenate(rows, axis=0)
    routed = jnp.dot(placed[:, :rec_dev], own[...], preferred_element_type=F32) + jnp.dot(
        placed[:, rec_dev:], other[...], preferred_element_type=F32
    )
    first = 0
    for block in transform(split(routed), even, odd):
        width = block.shape[1]
        block = block.astype(BF16).reshape(outs, aper // ROWS, ROWS, width)
        for r in range(outs):
            out[:, r, :, first : first + width] = block[r]
        first += width
    token[...] = jnp.zeros(token.shape, F32)


def sum_rows(values):
    row = lax.broadcasted_iota(I32, values[0].shape, 0)
    for shift in (4, 2, 1):
        upper = row % (2 * shift) < shift
        half = len(values) // 2
        joined = []
        for a, b in zip(values[:half], values[half:]):
            if shift == 4:
                rolled = pltpu.roll(jnp.where(upper, b, a), 4, 0)
            else:
                rolled = jnp.where(upper, pltpu.roll(a, 8 - shift, 0), pltpu.roll(b, shift, 0))
            joined.append(jnp.where(upper, a, b) + rolled)
        values = joined
    return values[0]


def products_kernel(chunks, count, with_total, extra, shares, *refs):
    pieces = refs[:count]
    even, odd, spectra = refs[count : count + 3]
    totals = refs[count + 3 : count + 3 + len(shares) * with_total]
    outs = refs[count + 3 + len(shares) * with_total + extra : -1]
    work = refs[-1]
    samples = work.shape[1]
    number = spectra.shape[1]
    rows = work.shape[0] // len(chunks)
    sources = rows // ROWS
    data = jnp.concatenate([x[...].reshape(-1, samples) for x in pieces], axis=0)
    first = 0
    for block in transform(split(data), even, odd):
        work[:, first : first + block.shape[1]] = block
        first += block.shape[1]
    if len(outs) > len(shares):
        outs[-1][...] = jnp.zeros(outs[-1].shape, F32)
    for start, distance, width in groups(samples):
        for block in range(width // 128):
            re = pl.ds(start + block * 128, 128)
            im = pl.ds(start + distance + block * 128, 128)
            sums = {}
            for c in range(len(chunks)):
                for r in [i * (number // 2) + k for i in shares for k in range(number // 2)]:
                    right = [spectra[chunks[c], r, :, k].astype(F32) for k in (re, im)]
                    for h in range(ROWS // 8):
                        b_re, b_im = (b[8 * h : 8 * h + 8] for b in right)
                        for s in range(sources):
                            top = c * rows + s * ROWS + h * 8
                            a_re, a_im = work[top : top + 8, re], work[top : top + 8, im]
                            x = a_re * b_re - a_im * b_im
                            y = a_re * b_im + a_im * b_re
                            if (s, r) in sums:
                                x, y = x + sums[s, r][0], y + sums[s, r][1]
                            sums[s, r] = (x, y)
            share = number // 2
            for n, i in enumerate(shares):
                keys = [(s, i * share + r) for r in range(share) for s in range(sources)]
                for part, columns in enumerate((re, im)):
                    value = sum_rows([sums[key][part] for key in keys])
                    if with_total:
                        value = value + totals[n][:, columns]
                    outs[n][:, columns] = value


def finish_kernel(scale, filters, mine, arrived, even, odd, out):
    count = even.shape[1]
    sources, out_dev, samples = out.shape
    raw = mine[...] + arrived[...]
    rows = raw.shape[0]
    dot = functools.partial(jnp.dot, preferred_element_type=F32)
    waves, column = [], 0
    for g, (start, distance, width) in enumerate(groups(samples)):
        g_re = filters[0:1, column : column + width] * scale
        g_im = filters[1:2, column : column + width] * scale
        column += width
        x = raw[:, start : start + width]
        y = raw[:, start + distance : start + distance + width]
        x, y = g_re * x - g_im * y, g_re * y + g_im * x
        if g < 2:
            waves.append(dot(jnp.concatenate([x, y], axis=1).astype(BF16), even[g]))
        else:
            both = dot(jnp.concatenate([x, y], axis=0).astype(BF16), odd[g - 2])
            waves.append(both[:rows, :count] - both[rows:, count:])
            waves.append(both[:rows, count:] + both[rows:, :count])
    a, b, h_re, h_im, v_re, v_im, w_re, w_im = waves
    root = math.sqrt(0.5)
    plus, minus = a + b, a - b
    u_re, u_im = v_re + w_re, v_im + w_im
    v_re, v_im = v_re - w_re, v_im - w_im
    less, more = root * (v_re - v_im), root * (v_re + v_im)
    results = (
        plus + h_re + u_re,
        minus - h_im + less,
        plus - h_re - u_im,
        minus + h_im - more,
        plus + h_re - u_re,
        minus - h_im - less,
        plus - h_re + u_im,
        minus + h_im + more,
    )
    for k, value in enumerate(results):
        value = value.reshape(out_dev, sources, count)
        for r in range(out_dev):
            out[:, r, k * count : (k + 1) * count] = value[r].astype(BF16)


def call(kernel, out_shape, kinds, scratch=(), limit=24, cost=1):
    spaces = {"s": pltpu.SMEM, "v": pltpu.VMEM, "a": pl.ANY}
    specs = [pl.BlockSpec(memory_space=spaces[k]) for k in kinds]
    return pl.pallas_call(
        kernel,
        out_shape=out_shape,
        in_specs=specs,
        out_specs=[pl.BlockSpec(memory_space=pltpu.VMEM)] * len(out_shape),
        cost_estimate=pl.CostEstimate(
            flops=cost * 10**9, transcendentals=0, bytes_accessed=cost * 3 * 10**6
        ),
        scratch_shapes=list(scratch),
        compiler_params=pltpu.CompilerParams(vmem_limit_bytes=limit << 20),
    )


def per_device(ring_size, source_traces, surface_filter, records, owners, aperture):
    sources, own_traces, samples = source_traces.shape
    out_dev, aper = aperture.shape
    rec_dev = records.shape[0]
    count = samples // 8
    struct = jax.ShapeDtypeStruct
    rx, xl = (lax.axis_index(axis).astype(I32).reshape(1) for axis in ("rx", "xl"))
    outs = 2 * out_dev
    chunks = aper // ROWS
    token = struct((8, 128), F32)

    def after(token, *values):
        return lax.optimization_barrier((*values, token))

    def swap(x):
        return lax.ppermute(x, "xl", [(0, 1), (1, 0)])

    notes = jnp.concatenate([owners.reshape(-1, aper), aperture], axis=0)
    table_shapes = [struct((2, count, count), BF16), struct((3, count, 2 * count), BF16)]
    fine = [pltpu.VMEM((2, FORWARD_STEP, 4 * count), F32)]
    tables = call(forward_kernel, table_shapes, "ss", fine)(rx, xl)

    ringed = ring_size == 8 and own_traces == ROWS and aper == 8 * ROWS

    def setup():
        return call(
            functools.partial(setup_kernel, own_traces, aper, ringed),
            [struct((chunks, outs, ROWS, samples), BF16), token],
            "ssvvvvvv",
            cost=4,
        )(rx, xl, records, swap(records), notes, swap(notes), *tables)

    def arrange(filters):
        return call(filters_kernel, [struct(filters.shape, F32)], "v")(filters)[0]

    def add(pieces, numbers, totals, extra=(), mark=True, shares=(0, 1)):
        kernel = functools.partial(
            products_kernel, numbers, len(pieces), bool(totals), len(extra), shares
        )
        arguments = [*pieces, *tables, spectra, *totals, *extra]
        row_shape = struct((out_dev * sources, samples), F32)
        result = call(
            kernel,
            [*[row_shape] * len(shares), *[token] * mark],
            "v" * len(arguments),
            [pltpu.VMEM((len(numbers) * sources * ROWS, samples), F32)],
        )(*arguments)
        return result[: len(shares)], result[-1]

    if ringed:
        order = [0, 2, 4, 6, 7, 5, 3, 1]
        same, cross = [], []
        for i in range(8):
            here, above, below = order[i], order[(i + 1) % 8], order[i - 1]
            same += [(2 * here, 2 * above), (2 * here + 1, 2 * below + 1)]
            cross += [(2 * here + 1, 2 * above), (2 * here, 2 * below + 1)]

        def send(x, pairs=same):
            return lax.ppermute(x, ("rx", "xl"), pairs)

        a1, b1 = send(source_traces), send(source_traces, cross)
        spectra, done = setup()
        a_held, first = after(done, a1)
        a2 = send(a_held)
        totals, done = add([source_traces], [0], [], [first])
        b_held, second = after(done, b1)
        b2 = send(b_held)
        totals, done = add([a1, b1], [1, 2], totals, [second])
        filters = arrange(surface_filter)
        a_held, first = after(done, a2)
        b_held, filters, second = after(done, b2, filters)
        a3, b3 = send(a_held), send(b_held)
        totals, _ = add([a2, b2], [3, 4], totals, [first, second], mark=False)
        a4 = send(a3)
        totals, _ = add([a3, b3], [5, 6], totals, mark=False)
        (theirs,), _ = add([a4], [7], totals[1:], mark=False, shares=(1,))
        (mine,), _ = add([a4], [7], totals[:1], mark=False, shares=(0,))
    else:
        spectra, _ = setup()
        gathered = lax.all_gather(source_traces, "rx", axis=1, tiled=True)
        parts = [gathered[:, k * ROWS : (k + 1) * ROWS] for k in range(chunks)]
        totals = []
        for k in range(0, chunks, 2):
            totals, _ = add(parts[k : k + 2], [k, k + 1], totals, mark=False)
        mine, theirs = totals
        filters = arrange(surface_filter)

    fine = [pltpu.VMEM((2, 5, INVERSE_STEP, count), F32)]
    inverse = call(inverse_kernel, table_shapes, "", fine)()
    return call(
        functools.partial(finish_kernel, 1.0 / math.sqrt(aper)),
        [struct((sources, out_dev, samples), BF16)],
        "vvvvv",
    )(filters, mine, swap(theirs), *inverse)[0]


def solution(mesh):
    in_specs = (
        P(None, ("groups", "rx", "xl"), None),
        P(),
        P(("groups", "rx", "xl"), None),
        P(("groups", "rx", "xl")),
        P(("groups", "rx", "xl"), None),
    )
    out_specs = P(None, ("groups", "rx", "xl"), None)
    return jax.shard_map(
        functools.partial(per_device, mesh.shape["rx"]),
        mesh=mesh,
        in_specs=in_specs,
        out_specs=out_specs,
        check_vma=False,
    )
```
